512 devices in a mesh: row: 8 (over x, y_lo), col: 32 (over y_hi, z), img: 2 (over core).
Axes of the slice: x: 4, y: 4 (y_hi: 2, y_lo: 2; y = y_hi * 2 + y_lo), z: 16, core: 2. Of those that a mesh axis runs over, the one named last changes fastest.
Arguments:
- x_in: bfloat16 [2, 256, 256, 1536], P('img', 'row', 'col'), may hold values from -6 to 6
- gate_in: bfloat16 [2, 256, 256, 1536], P('img', 'row', 'col'), may hold values from -6 to 6
- proj_bc: bfloat16 [2, 256, 256, 64], P('img', 'row', 'col'), may hold values from -3 to 3
- dt_raw: bfloat16 [2, 256, 256, 48], P('img', 'row', 'col'), may hold values from -3 to 3
- step_index: int32 [2], P('img'), may hold values from 0 to 999
- step_table: float32 [1000, 48], replicated, may hold values from -1.5 to 0.5
- rates: float32 [2, 24], replicated, may hold values from 0.000390625 to 0.046875, as said below
- skip: float32 [24], replicated, may hold values from 0.5 to 2
- norm_gain: float32 [1536], replicated, may hold values from 0.5 to 1.5
Outputs:
- mixed: bfloat16 [2, 256, 256, 1536], P('img', 'row', 'col')
The draws below stay inside these ranges and needn't reach their ends.
Inputs may be any that keep to these rules, and one draw needn't show every extreme that they name: rates of the row heads are given per column step and those of the column heads per row step.
All inputs are finite; a program needn't handle non-finite values.
Results may differ from the reference program's by a relative error of at most 0.0065.
Values may be sent and summed in bfloat16 or wider, within the bound.
A program may use at most 128 MiB of HBM per device.

```python
import math
import jax
import jax.numpy as jnp
from jax import lax

HEADS = 24
HEAD = 64
STATE = 16
STEPS = 1000
INNER = 1536
BATCH = 2
H = 256
W = 256


def draw_rates(key, part):
    lengths = jnp.array([W, H], jnp.float32)[:, None]
    spread = jax.random.uniform(key, (2, HEADS), jnp.float32)
    lowest, highest = (0.3, 12.0)
    return jnp.exp(jnp.log(lowest) + spread * (jnp.log(highest) - jnp.log(lowest))) / lengths


def steps_of(rng, dims, shards, least, largest):
    def one(dim, blocks):
        heights = jax.random.uniform(jax.random.fold_in(jax.random.fold_in(rng, 6), dim), (blocks,), jnp.float32, least / len(shards), largest / len(shards))
        return jnp.repeat(jnp.exp(heights), dims[dim] // blocks).reshape((-1,) + (1,) * (len(dims) - dim - 1))

    level = one(*shards[0])
    for cut in shards[1:]:
        level = level * one(*cut)
    return level


def scatter_about(own_key, dims, scale, reach, pieces=(), dtype=jnp.bfloat16):
    loudness = steps_of(own_key, dims, pieces, -0.22, 0.18) if pieces else 1.0
    values = jax.random.normal(own_key, dims, jnp.float32) * scale * loudness
    return jnp.minimum(jnp.maximum(values, -reach), reach).astype(dtype)


def setup_inputs(seed: int = 0) -> dict:
    arg_keys = jax.random.split(jax.random.key(seed), 10)
    return {
        "x_in": scatter_about(arg_keys[0], (BATCH, H, W, INNER), 1.0, 6.0, ((0, 2), (1, 8), (2, 32))),
        "gate_in": scatter_about(arg_keys[1], (BATCH, H, W, INNER), 1.0, 6.0, ((0, 2), (1, 8), (2, 32))),
        "proj_bc": scatter_about(arg_keys[2], (BATCH, H, W, 4 * STATE), 0.5, 3.0, ((0, 2), (1, 8), (2, 32))),
        "dt_raw": scatter_about(arg_keys[3], (BATCH, H, W, 2 * HEADS), 0.5, 3.0, ((0, 2), (1, 8), (2, 32))),
        "step_index": jax.random.randint(arg_keys[4], (BATCH,), 0, STEPS).astype(jnp.int32),
        "step_table": jnp.clip(jax.random.uniform(arg_keys[5], (STEPS, 2 * HEADS), jnp.float32, -1.5, 0.5), -1.5, 0.5),
        "rates": draw_rates(jax.random.fold_in(arg_keys[9], 71), 0),
        "skip": jnp.clip(jnp.exp(jax.random.uniform(arg_keys[7], (HEADS,), jnp.float32, math.log(0.5), math.log(2.0))), 0.5, 2.0),
        "norm_gain": jnp.clip(1.0 + 0.1 * jax.random.normal(arg_keys[8], (INNER,), jnp.float32), 0.5, 1.5),
    }


def line_scan(inputs, decay_log, in_map, out_map):

    def advance(state_now, items):
        token_in, token_decay, token_b, token_c = items
        state_now = jnp.exp(token_decay)[:, :, None, None] * state_now + token_in[:, :, :, None] * token_b[:, None, None, :]
        result = jnp.einsum('lhpn,ln->lhp', state_now, token_c, precision=lax.Precision.HIGHEST)
        return (state_now, result)
    line_count = inputs.shape[0]
    start = jnp.zeros((line_count, HEADS, HEAD, STATE), jnp.float32)
    items = (jnp.moveaxis(inputs, 1, 0), jnp.moveaxis(decay_log, 1, 0), jnp.moveaxis(in_map, 1, 0), jnp.moveaxis(out_map, 1, 0))
    final, results = lax.scan(advance, start, items)
    return jnp.moveaxis(results, 0, 1)

def reference(x_in, gate_in, proj_bc, dt_raw, step_index, step_table, rates, skip, norm_gain):
    bias = step_table[step_index]
    step_size = jax.nn.softplus(dt_raw.astype(jnp.float32) + bias[:, None, None, :])
    decay_log = -rates.reshape(2 * HEADS) * step_size
    x_heads = x_in.astype(jnp.float32).reshape(BATCH, H, W, HEADS, HEAD)
    u_row = (step_size[..., :HEADS, None] * x_heads).astype(jnp.bfloat16)
    u_col = (step_size[..., HEADS:, None] * x_heads).astype(jnp.bfloat16)
    maps = proj_bc.astype(jnp.float32)
    y_row = line_scan(u_row.astype(jnp.float32).reshape(BATCH * H, W, HEADS, HEAD), decay_log[..., :HEADS].reshape(BATCH * H, W, HEADS), maps[..., :STATE].reshape(BATCH * H, W, STATE), maps[..., STATE:2 * STATE].reshape(BATCH * H, W, STATE))
    y_row = y_row.astype(jnp.bfloat16).reshape(BATCH, H, W, HEADS, HEAD)
    y_col = line_scan(jnp.swapaxes(u_col.astype(jnp.float32), 1, 2).reshape(BATCH * W, H, HEADS, HEAD), jnp.swapaxes(decay_log[..., HEADS:], 1, 2).reshape(BATCH * W, H, HEADS), jnp.swapaxes(maps[..., 2 * STATE:3 * STATE], 1, 2).reshape(BATCH * W, H, STATE), jnp.swapaxes(maps[..., 3 * STATE:], 1, 2).reshape(BATCH * W, H, STATE))
    y_col = jnp.swapaxes(y_col.astype(jnp.bfloat16).reshape(BATCH, W, H, HEADS, HEAD), 1, 2)
    gate = jax.nn.silu(gate_in.astype(jnp.float32).reshape(BATCH, H, W, HEADS, HEAD))
    mixed = (y_row.astype(jnp.float32) + y_col.astype(jnp.float32) + skip[:, None] * x_heads) * gate
    power = lax.optimization_barrier(jnp.mean(mixed * mixed, axis=(-2, -1), keepdims=True))
    normed = mixed * lax.rsqrt(power + 1e-05) * norm_gain.reshape(HEADS, HEAD)
    return normed.astype(jnp.bfloat16).reshape(BATCH, H, W, HEADS * HEAD)
```

```python
import functools

import jax
import jax.numpy as jnp
from jax import lax
from jax.experimental import pallas as pl
from jax.experimental.pallas import tpu as pltpu
from jax.sharding import PartitionSpec as P

HEADS = 24
HEAD = 64
STATE = 16
INNER = HEADS * HEAD
GROUPS = 4
LOG2E = 1.4426950408889634
F32 = jnp.float32
BF16 = jnp.bfloat16


def dot(a, b):
    return jnp.dot(a, b, preferred_element_type=F32)


def split(v, pieces):
    parts = []
    for _ in range(pieces):
        part = v.astype(BF16)
        parts.append(part)
        v = v - part.astype(F32)
    return parts


def dot_exact(zero_one, v, pieces=3):
    return sum(dot(zero_one, part) for part in split(v, pieces))


def expand(v, heads_to_channels, pieces=2):
    return sum(dot(part, heads_to_channels) for part in split(v, pieces))


def softplus(v):
    return jnp.maximum(v, 0.0) + jnp.log(1.0 + jnp.exp(-jnp.abs(v)))


def kernel(
    lanes, tall, step_ref, table_ref, rates_ref, skip_ref, gain_ref, x_ref, gate_ref, bc_ref, dt_ref, out_ref,
    got_x, got_bc, got_dt, y_send, got_y, f_send, got_f, t_send, got_t, s_send, got_s, w_row, u_row_s, acc, act, mixed,
    x_out, x_in, m_out, m_in, y_out, y_in, f_out, f_in, s_out, s_in,
):
    tokens = lanes * 8
    half = tokens // 2
    ring = lanes // 2
    group = INNER // GROUPS
    group_heads = HEADS // GROUPS
    me_col = lax.axis_index("col")
    me_row = lax.axis_index("row")
    hi, z = me_col // ring, me_col % ring

    offsets = []
    for k in range(ring):
        m = (k + 1) // 2
        dz = (ring // 2 - m) if k % 2 else -(ring // 2 - m)
        offsets += [(1, dz), (0, dz)]
    offsets = [o for o in offsets if o != (0, 0)]
    col_peers = [((hi + dy) % 2) * ring + (z + dz + ring) % ring for dy, dz in offsets]
    row_peers = [(me_row + k) % tall for k in range(1, tall)]

    barrier = pltpu.get_barrier_semaphore()
    for p in col_peers:
        pl.semaphore_signal(barrier, inc=1, device_id={"col": p}, device_id_type=pl.DeviceIdType.MESH)
    for q in row_peers:
        pl.semaphore_signal(barrier, inc=1, device_id={"row": q}, device_id_type=pl.DeviceIdType.MESH)

    def send_col(src, dst, out_sem, in_sem, p):
        pltpu.make_async_remote_copy(
            src_ref=src, dst_ref=dst, send_sem=out_sem, recv_sem=in_sem,
            device_id={"col": p}, device_id_type=pl.DeviceIdType.MESH,
        ).start()

    def send_row(src, dst, out_sem, in_sem, q):
        pltpu.make_async_remote_copy(
            src_ref=src, dst_ref=dst, send_sem=out_sem, recv_sem=in_sem,
            device_id={"row": q}, device_id_type=pl.DeviceIdType.MESH,
        ).start()

    def wait_for(ref, sem):
        pltpu.make_async_copy(ref, ref, sem).wait()

    rows = lax.broadcasted_iota(jnp.int32, (tokens, tokens), 0)
    cols = lax.broadcasted_iota(jnp.int32, (tokens, tokens), 1)
    causal = rows >= cols
    same = causal & ((rows & 7) == (cols & 7))
    channel = lax.broadcasted_iota(jnp.int32, (HEADS, INNER), 1)
    head = lax.broadcasted_iota(jnp.int32, (HEADS, INNER), 0)
    spread = ((channel >= head * HEAD) & (channel < (head + 1) * HEAD)).astype(BF16)
    bias = table_ref[pl.ds(step_ref[0], 1), :]

    dt_own = dt_ref[...].astype(F32).reshape(tokens, 2 * HEADS)
    dt_col = softplus(dt_own[:, HEADS:] + bias[:, HEADS:])
    log_col = dt_col * (-LOG2E * rates_ref[1:2, :])
    run_col = dot_exact(same.astype(BF16), log_col)
    run3 = run_col.reshape(lanes, 8, HEADS)
    end_col = run3[lanes - 1]
    to_end = jnp.exp2(end_col[None] - run3).reshape(tokens, HEADS)
    x_all = x_ref[...].astype(F32).reshape(tokens, INNER)
    u_col = (expand(dt_col, spread) * x_all).astype(BF16)
    bc_own = bc_ref[...].astype(F32).reshape(tokens, 4 * STATE)
    b_col = bc_own[:, 2 * STATE : 3 * STATE].astype(BF16)
    c_col = bc_own[:, 3 * STATE :].astype(BF16)
    wide = 8 * STATE
    fan = (
        (lax.broadcasted_iota(jnp.int32, (STATE, wide), 1) & (STATE - 1))
        == lax.broadcasted_iota(jnp.int32, (STATE, wide), 0)
    ).astype(BF16)
    own_col = (lax.broadcasted_iota(jnp.int32, (tokens, wide), 1) // STATE) == (
        lax.broadcasted_iota(jnp.int32, (tokens, wide), 0) & 7
    )
    b_wide = jnp.where(own_col, dot(b_col, fan), 0.0)
    c_wide = jnp.where(own_col, dot(c_col, fan), 0.0).astype(BF16)
    u_end = (expand(to_end, spread) * u_col.astype(F32)).astype(BF16)
    states = dot(b_wide.T.astype(BF16), u_end)
    f_send[...] = states.astype(BF16).reshape(8, STATE, INNER)
    t_send[...] = jnp.concatenate([end_col, jnp.zeros((8, 128 - HEADS), F32)], axis=1)

    pl.semaphore_wait(barrier, lanes - 1 + tall - 1)

    for p in col_peers:
        send_col(bc_ref.at[p], got_bc.at[me_col], m_out, m_in.at[0], p)
        send_col(dt_ref.at[p], got_dt.at[me_col], m_out, m_in.at[1], p)
    for q in row_peers:
        send_row(f_send.at[q], got_f.at[me_row], f_out.at[0], f_in.at[0], q)
        send_row(t_send, got_t.at[me_row], f_out.at[1], f_in.at[1], q)
    for g in range(GROUPS):
        part = pl.ds(g * group, group)
        for p in col_peers:
            send_col(x_ref.at[p, :, part], got_x.at[me_col, :, part], x_out.at[g], x_in.at[g], p)
    got_bc[me_col] = bc_ref[me_col]
    got_dt[me_col] = dt_ref[me_col]
    got_x[me_col] = x_ref[me_col]
    got_f[me_row] = f_send[me_row]
    got_t[me_row] = t_send[...]

    def weights_of(run, run_t, scores, bar, h):
        top = jnp.exp2(run[:half, h : h + 1] - run_t[h : h + 1, :half] + bar[:half, :half]) * scores[:half, :half]
        low = jnp.exp2(run[half:, h : h + 1] - run_t[h : h + 1, :] + bar[half:, :]) * scores[half:, :]
        return top.astype(BF16), low.astype(BF16)

    def transposed(run):
        return jnp.concatenate([run, jnp.zeros((tokens, 128 - HEADS), F32)], axis=1).T

    def scores_of(c, b):
        return lax.dot_general(c, b, (((1,), (1,)), ((), ())), preferred_element_type=F32)

    lane = lax.broadcasted_iota(jnp.int32, (1, 128), 1)

    bar_col = jnp.where(same, 0.0, -1e30)
    scores_col = scores_of(c_col, b_col)
    run_col_t = transposed(run_col)
    skip_wide = expand(skip_ref[...], spread, 3)
    for pair in range(HEADS // 2):
        part = slice(pair * 128, pair * 128 + 128)
        top0, low0 = weights_of(run_col, run_col_t, scores_col, bar_col, 2 * pair)
        top1, low1 = weights_of(run_col, run_col_t, scores_col, bar_col, 2 * pair + 1)
        u = u_col[:, part]
        kept = skip_wide[:, part] * x_all[:, part]
        acc[:half, part] = jnp.where(lane < HEAD, dot(top0, u[:half]), dot(top1, u[:half])) + kept[:half]
        acc[half:, part] = jnp.where(lane < HEAD, dot(low0, u), dot(low1, u)) + kept[half:]

    wait_for(got_f.at[pl.ds(0, tall - 1)], f_in.at[0])
    wait_for(got_t.at[pl.ds(0, tall - 1)], f_in.at[1])
    ends = jnp.concatenate([got_t[k, pl.ds(me_row, 1), :] for k in range(tall)], axis=0)
    decay = expand(jnp.exp2(ends[:, :HEADS]), spread, 3)
    carry = jnp.zeros((STATE, INNER), F32)
    for k in range(tall):
        s_send[k] = carry.astype(BF16)
        if k < tall - 1:
            carry = decay[k : k + 1] * carry + got_f[k].astype(F32)

    wait_for(got_bc.at[pl.ds(0, lanes - 1)], m_in.at[0])
    wait_for(got_dt.at[pl.ds(0, lanes - 1)], m_in.at[1])
    for q in row_peers:
        send_row(s_send.at[q], got_s.at[me_row], s_out, s_in, q)
    got_s[me_row] = s_send[me_row]
    bc_line = got_bc[...].astype(F32).reshape(tokens, 4 * STATE)
    dt_line = got_dt[...].astype(F32).reshape(tokens, 2 * HEADS)
    dt_row = softplus(dt_line[:, :HEADS] + bias[:, :HEADS])
    run_row = dot_exact(causal.astype(BF16), dt_row * (-LOG2E * rates_ref[0:1, :]))
    run_row_t = transposed(run_row)
    scores_row = scores_of(bc_line[:, STATE : 2 * STATE].astype(BF16), bc_line[:, :STATE].astype(BF16))
    bar_row = jnp.where(causal, 0.0, -1e30)
    u_row_s[...] = expand(dt_row, spread)
    for h in range(HEADS):
        top, low = weights_of(run_row, run_row_t, scores_row, bar_row, h)
        w_row[h, :half, :half] = top
        w_row[h, half:, :] = low

    gate = gate_ref[...].astype(F32).reshape(tokens, INNER)
    act[...] = 0.5 * gate * (1.0 + jnp.tanh(0.5 * gate))

    wait_for(got_s.at[pl.ds(0, tall - 1)], s_in)
    entering = dot(c_wide, got_s[...].astype(F32).reshape(wide, INNER).astype(BF16))
    acc[...] += expand(jnp.exp2(run_col), spread) * entering

    for g in range(GROUPS):
        part = pl.ds(g * group, group)
        wait_for(got_x.at[pl.ds(0, lanes - 1), :, part], x_in.at[g])
        x_line = got_x[:, :, part].astype(F32).reshape(tokens, group)
        u = (u_row_s[:, part] * x_line).astype(BF16)
        for i in range(group_heads // 2):
            h = g * group_heads + 2 * i
            u_pair = u[:, i * 128 : i * 128 + 128]
            top = jnp.where(
                lane < HEAD, dot(w_row[h, :half, :half], u_pair[:half]), dot(w_row[h + 1, :half, :half], u_pair[:half])
            )
            low = jnp.where(lane < HEAD, dot(w_row[h, half:, :], u_pair), dot(w_row[h + 1, half:, :], u_pair))
            here = pl.ds(h * HEAD, 128)
            y_send[: lanes // 2, :, here] = top.reshape(lanes // 2, 8, 128).astype(BF16)
            y_send[lanes // 2 :, :, here] = low.reshape(lanes // 2, 8, 128).astype(BF16)
        for p in col_peers:
            send_col(y_send.at[p, :, part], got_y.at[me_col, :, part], y_out.at[g], y_in.at[g], p)
        got_y[me_col, :, part] = y_send[me_col, :, part]

    power = jnp.zeros((tokens, 128), F32)
    for g in range(GROUPS):
        part = pl.ds(g * group, group)
        wait_for(got_y.at[pl.ds(0, lanes - 1), :, part], y_in.at[g])
        y_row = got_y[:, :, part].astype(F32).reshape(tokens, group)
        v = (y_row + acc[:, part]) * act[:, part]
        mixed[:, part] = v
        for i in range(group // 128):
            w = v[:, i * 128 : i * 128 + 128]
            power += w * w
    scale = lax.rsqrt(jnp.sum(power, axis=1, keepdims=True) * (1.0 / INNER) + 1e-05)
    out_ref[...] = (mixed[...] * scale * gain_ref[...]).reshape(lanes, 8, INNER).astype(BF16)

    wait_for(bc_ref.at[pl.ds(0, lanes - 1)], m_out)
    wait_for(dt_ref.at[pl.ds(0, lanes - 1)], m_out)
    wait_for(f_send.at[pl.ds(0, tall - 1)], f_out.at[0])
    wait_for(got_t.at[pl.ds(0, tall - 1)], f_out.at[1])
    wait_for(s_send.at[pl.ds(0, tall - 1)], s_out)
    for g in range(GROUPS):
        part = pl.ds(g * group, group)
        wait_for(x_ref.at[pl.ds(0, lanes - 1), :, part], x_out.at[g])
        wait_for(y_send.at[pl.ds(0, lanes - 1), :, part], y_out.at[g])


def body(lanes, tall, x_in, gate_in, proj_bc, dt_raw, step_index, step_table, rates, skip, norm_gain):
    tokens = lanes * 8
    vmem = pl.BlockSpec(memory_space=pltpu.VMEM)
    smem = pl.BlockSpec(memory_space=pltpu.SMEM)
    dma = pltpu.SemaphoreType.DMA
    out = pl.pallas_call(
        functools.partial(kernel, lanes, tall),
        out_shape=jax.ShapeDtypeStruct((lanes, 8, INNER), BF16),
        in_specs=[smem] + [vmem] * 8,
        out_specs=vmem,
        scratch_shapes=[
            pltpu.VMEM((lanes, 8, INNER), BF16),
            pltpu.VMEM((lanes, 8, 4 * STATE), BF16),
            pltpu.VMEM((lanes, 8, 2 * HEADS), BF16),
            pltpu.VMEM((lanes, 8, INNER), BF16),
            pltpu.VMEM((lanes, 8, INNER), BF16),
            pltpu.VMEM((8, STATE, INNER), BF16),
            pltpu.VMEM((tall, STATE, INNER), BF16),
            pltpu.VMEM((8, 128), F32),
            pltpu.VMEM((tall, 8, 128), F32),
            pltpu.VMEM((tall, STATE, INNER), BF16),
            pltpu.VMEM((8, STATE, INNER), BF16),
            pltpu.VMEM((HEADS, tokens, tokens), BF16),
            pltpu.VMEM((tokens, INNER), F32),
            pltpu.VMEM((tokens, INNER), F32),
            pltpu.VMEM((tokens, INNER), F32),
            pltpu.VMEM((tokens, INNER), F32),
            dma((GROUPS,)),
            dma((GROUPS,)),
            dma,
            dma((2,)),
            dma((GROUPS,)),
            dma((GROUPS,)),
            dma((2,)),
            dma((2,)),
            dma,
            dma,
        ],
        compiler_params=pltpu.CompilerParams(
            collective_id=0, has_side_effects=True, vmem_limit_bytes=60 * 1024 * 1024
        ),
    )(
        step_index,
        step_table,
        rates,
        skip.reshape(1, HEADS),
        norm_gain.reshape(1, INNER),
        x_in.reshape(lanes, 8, INNER),
        gate_in.reshape(lanes, 8, INNER),
        proj_bc.reshape(lanes, 8, 4 * STATE),
        dt_raw.reshape(lanes, 8, 2 * HEADS),
    )
    return out.reshape(1, lanes, 8, INNER)


def solution(mesh):
    tile = P("img", "row", "col", None)
    return jax.shard_map(
        functools.partial(body, mesh.shape["col"], mesh.shape["row"]),
        mesh=mesh,
        in_specs=(tile, tile, tile, tile, P("img"), P(), P(), P(), P()),
        out_specs=tile,
        check_vma=False,
    )
```

```python
import functools

import jax
import jax.numpy as jnp
from jax import lax
from jax.experimental import pallas as pl
from jax.experimental.pallas import tpu as pltpu
from jax.sharding import PartitionSpec as P

HEADS = 24
HEAD = 64
STATE = 16
INNER = HEADS * HEAD
GROUPS = 4
WINDOW = 8
AHEAD = 2
LOG2E = 1.4426950408889634
F32 = jnp.float32
BF16 = jnp.bfloat16


def dot(a, b):
    return jnp.dot(a, b, preferred_element_type=F32)


def split(v, pieces):
    parts = []
    for _ in range(pieces):
        part = v.astype(BF16)
        parts.append(part)
        v = v - part.astype(F32)
    return parts


def dot_exact(zero_one, v, pieces=3):
    return sum(dot(zero_one, part) for part in split(v, pieces))


def expand(v, heads_to_channels, pieces=2):
    return sum(dot(part, heads_to_channels) for part in split(v, pieces))


def softplus(v):
    return jnp.maximum(v, 0.0) + jnp.log(1.0 + jnp.exp(-jnp.abs(v)))


def kernel(
    lanes, tall, step_ref, table_hbm, rates_ref, skip_ref, gain_ref, x_hbm, gate_hbm, bc_hbm, dt_hbm, out_ref,
    table_ref, x_ref, gate_ref, bc_ref, dt_ref, load_sem,
    got_x, got_bc, got_dt, y_send, got_y, f_send, got_f, t_send, got_t, s_send, got_s,
    l_send, got_l, i_send, got_i, e_send, got_e, w_row, u_row_s, end_s, near, acc, act, mixed,
    x_out, x_in, m_out, m_in, y_out, y_in, f_out, f_in, s_out, s_in, l_out, l_in, i_out, i_in, e_out, e_in,
):
    tile_rows = x_ref.shape[0]
    tokens = tile_rows * 8
    half = tokens // 2
    windows = lanes // WINDOW
    lines = tile_rows // WINDOW
    group = INNER // GROUPS
    group_heads = HEADS // GROUPS
    middle = WINDOW // 2
    me_col = lax.axis_index("col")
    me_row = lax.axis_index("row")

    def around(c):
        return (c + 2 * lanes) % lanes

    def rows_of(c):
        return pl.ds(((c + middle) % WINDOW) * lines, lines)

    order = sorted(range(1, middle + 1), reverse=True)
    to = [d for k in order for d in ((k, -k) if k < middle else (k,))]
    fro = [d for k in order for d in ((-k, k) if k < middle else (-k,))]
    row_peers = [(me_row + k) % tall for k in range(1, tall)]
    after, before, across = around(me_col + WINDOW), around(me_col - WINDOW), around(me_col + 2 * WINDOW)
    place = ((me_col + middle - 1) % lanes) // WINDOW
    cut = around(middle - me_col)
    cut_in = jnp.where(place == 0, cut, WINDOW)
    cut_out = jnp.where(place == 0, cut, 0)

    barrier = pltpu.get_barrier_semaphore()

    def greet(**device):
        pl.semaphore_signal(barrier, inc=1, device_id=device, device_id_type=pl.DeviceIdType.MESH)

    near_set = sorted(set(to) | set(fro))
    for d in near_set:
        greet(col=around(me_col + d))
    for c in (after, before, across):
        greet(col=c)
    for q in row_peers:
        greet(row=q)

    loads = []
    for i, (src, dst) in enumerate(
        ((bc_hbm, bc_ref), (dt_hbm, dt_ref), (table_hbm, table_ref), (x_hbm, x_ref), (gate_hbm, gate_ref))
    ):
        loads.append(pltpu.make_async_copy(src, dst, load_sem.at[i]))
        loads[-1].start()

    def send_col(src, dst, out_sem, in_sem, p):
        pltpu.make_async_remote_copy(
            src_ref=src, dst_ref=dst, send_sem=out_sem, recv_sem=in_sem,
            device_id={"col": p}, device_id_type=pl.DeviceIdType.MESH,
        ).start()

    def send_row(src, dst, out_sem, in_sem, q):
        pltpu.make_async_remote_copy(
            src_ref=src, dst_ref=dst, send_sem=out_sem, recv_sem=in_sem,
            device_id={"row": q}, device_id_type=pl.DeviceIdType.MESH,
        ).start()

    def wait_for(ref, sem):
        pltpu.make_async_copy(ref, ref, sem).wait()

    rows = lax.broadcasted_iota(jnp.int32, (tokens, tokens), 0)
    cols = lax.broadcasted_iota(jnp.int32, (tokens, tokens), 1)
    causal = rows >= cols
    same = causal & ((rows & 7) == (cols & 7))
    channel = lax.broadcasted_iota(jnp.int32, (HEADS, INNER), 1)
    head = lax.broadcasted_iota(jnp.int32, (HEADS, INNER), 0)
    spread = ((channel >= head * HEAD) & (channel < (head + 1) * HEAD)).astype(BF16)

    def widen(v, kept, count):
        wide = count * STATE
        fan = (
            (lax.broadcasted_iota(jnp.int32, (STATE, wide), 1) & (STATE - 1))
            == lax.broadcasted_iota(jnp.int32, (STATE, wide), 0)
        ).astype(BF16)
        return jnp.where(kept, dot(v, fan), 0.0)

    for i in range(4):
        loads[i].wait()
    chosen = (lax.broadcasted_iota(jnp.int32, (8, table_ref.shape[1]), 1) == step_ref[0]).astype(BF16)
    bias = sum(
        lax.dot_general(chosen, part, (((1,), (1,)), ((), ())), preferred_element_type=F32)
        for part in split(table_ref[...], 3)
    )[0:1]
    dt_own = dt_ref[...].astype(F32).reshape(tokens, 2 * HEADS)
    dt_col = softplus(dt_own[:, HEADS:] + bias[:, HEADS:])
    log_col = dt_col * (-LOG2E * rates_ref[1:2, :])
    run_col = dot_exact(same.astype(BF16), log_col)
    run3 = run_col.reshape(tile_rows, 8, HEADS)
    end_col = run3[tile_rows - 1]
    to_end = jnp.exp2(end_col[None] - run3).reshape(tokens, HEADS)
    x_all = x_ref[...].astype(F32).reshape(tokens, INNER)
    u_col = (expand(dt_col, spread) * x_all).astype(BF16)
    bc_own = bc_ref[...].astype(F32).reshape(tokens, 4 * STATE)
    b_col = bc_own[:, 2 * STATE : 3 * STATE].astype(BF16)
    c_col = bc_own[:, 3 * STATE :].astype(BF16)
    own_col = (lax.broadcasted_iota(jnp.int32, (tokens, 8 * STATE), 1) // STATE) == (
        lax.broadcasted_iota(jnp.int32, (tokens, 8 * STATE), 0) & 7
    )
    c_wide = widen(c_col, own_col, 8).astype(BF16)
    u_end = (expand(to_end, spread) * u_col.astype(F32)).astype(BF16)
    states = dot(widen(b_col, own_col, 8).T.astype(BF16), u_end)
    f_send[...] = states.astype(BF16).reshape(8, STATE, INNER)
    t_send[...] = jnp.concatenate([end_col, jnp.zeros((8, 128 - HEADS), F32)], axis=1)

    def send_tokens(g):
        part = pl.ds(g * group, group)
        for d in to:
            c = around(me_col + d)
            send_col(x_ref.at[rows_of(c), :, part], got_x.at[middle - d, :, :, part], x_out.at[g], x_in.at[g], c)

    pl.semaphore_wait(barrier, len(near_set) + 3 + tall - 1)

    for d in to:
        c = around(me_col + d)
        send_col(bc_ref.at[rows_of(c)], got_bc.at[middle - d], m_out.at[0], m_in.at[0], c)
        send_col(dt_ref.at[rows_of(c)], got_dt.at[middle - d], m_out.at[1], m_in.at[1], c)
    for g in range(AHEAD):
        send_tokens(g)
    for q in row_peers:
        send_row(f_send.at[q], got_f.at[me_row], f_out.at[0], f_in.at[0], q)
        send_row(t_send, got_t.at[me_row], f_out.at[1], f_in.at[1], q)
    got_bc[middle] = bc_ref[rows_of(me_col)]
    got_dt[middle] = dt_ref[rows_of(me_col)]
    got_x[middle] = x_ref[rows_of(me_col)]
    got_f[me_row] = f_send[me_row]
    got_t[me_row] = t_send[...]

    def wait_near(ref, sem):
        wait_for(ref.at[pl.ds(0, WINDOW - 1)], sem)

    def weights_of(run, run_t, scores, bar, h):
        top = jnp.exp2(run[:half, h : h + 1] - run_t[h : h + 1, :half] + bar[:half, :half]) * scores[:half, :half]
        low = jnp.exp2(run[half:, h : h + 1] - run_t[h : h + 1, :] + bar[half:, :]) * scores[half:, :]
        return top.astype(BF16), low.astype(BF16)

    def transposed(run):
        return jnp.concatenate([run, jnp.zeros((tokens, 128 - HEADS), F32)], axis=1).T

    def scores_of(c, b):
        return lax.dot_general(c, b, (((1,), (1,)), ((), ())), preferred_element_type=F32)

    lane = lax.broadcasted_iota(jnp.int32, (1, 128), 1)

    wait_near(got_bc, m_in.at[0])
    wait_near(got_dt, m_in.at[1])
    line_size = 8 * lines
    tile_i, tile_j = rows // line_size, cols // line_size
    line_i, line_j = (rows // 8) % lines, (cols // 8) % lines
    joined = causal & (line_i == line_j) & ((tile_i >= cut_out) == (tile_j >= cut_out))
    bc_line = got_bc[...].astype(F32).reshape(tokens, 4 * STATE)
    dt_line = got_dt[...].astype(F32).reshape(tokens, 2 * HEADS)
    dt_row = softplus(dt_line[:, :HEADS] + bias[:, :HEADS])
    log_row = dt_row * (-LOG2E * rates_ref[0:1, :])
    run_row = dot_exact(joined.astype(BF16), log_row)
    ends_row = run_row.reshape(WINDOW, lines, 8, HEADS)[WINDOW - 1, :, 7:8, :]
    run4 = run_row.reshape(WINDOW, lines, 8, HEADS)
    tile4 = lax.broadcasted_iota(jnp.int32, (WINDOW, lines, 8, HEADS), 0)
    to_end_row = jnp.where(tile4 >= cut_out, jnp.exp2(ends_row[None] - run4), 0.0).reshape(tokens, HEADS)
    from_start = jnp.where(tile4 < cut_in, jnp.exp2(run4), 0.0).reshape(tokens, HEADS)
    own_line = (lax.broadcasted_iota(jnp.int32, (tokens, lines * STATE), 1) // STATE) == (
        lax.broadcasted_iota(jnp.int32, (tokens, lines * STATE), 0) // 8
    ) % lines
    b_row = bc_line[:, :STATE].astype(BF16)
    c_row = bc_line[:, STATE : 2 * STATE].astype(BF16)
    b_lines = widen(b_row, own_line, lines).T.astype(BF16)
    c_lines = widen(c_row, own_line, lines).astype(BF16)
    u_row_s[...] = expand(dt_row, spread)
    end_s[...] = expand(to_end_row, spread)
    line_decay = jnp.exp2(ends_row.reshape(lines, HEADS))
    e_send[...] = jnp.concatenate(
        [
            jnp.concatenate([line_decay, jnp.zeros((8 - lines, HEADS), F32)], axis=0),
            jnp.zeros((8, 128 - HEADS), F32),
        ],
        axis=1,
    )
    own_decay = expand(line_decay, spread, 3)
    send_col(e_send, got_e, e_out, e_in, after)
    scores_row = scores_of(c_row, b_row)
    run_row_t = transposed(run_row)
    bar_row = jnp.where(joined, 0.0, -1e30)
    for h in range(HEADS):
        top, low = weights_of(run_row, run_row_t, scores_row, bar_row, h)
        w_row[h, :half, :half] = top
        w_row[h, half:, :] = low

    def enter(g):
        part = pl.ds(g * group, group)
        wait_near(got_x.at[:, :, :, part], x_in.at[g])
        x_line = got_x[:, :, :, part].astype(F32).reshape(tokens, group)
        u = (u_row_s[:, part] * x_line).astype(BF16)
        u_end = (end_s[:, part] * u.astype(F32)).astype(BF16)
        state = dot(b_lines, u_end)
        l_send[:, :, part] = state.reshape(lines, STATE, group).astype(BF16)
        send_col(l_send.at[:, :, part], got_l.at[:, :, part], l_out.at[g], l_in.at[g], after)

        @pl.when((place == 0) | (place == windows - 1))
        def _():
            i_send[:, :, part] = state.reshape(lines, STATE, group).astype(BF16)
            pass_on(g)

        if g + AHEAD < GROUPS:
            send_tokens(g + AHEAD)
        for i in range(group_heads // 2):
            h = g * group_heads + 2 * i
            u_pair = u[:, i * 128 : i * 128 + 128]
            here = pl.ds(h * HEAD, 128)
            near[:half, here] = jnp.where(
                lane < HEAD, dot(w_row[h, :half, :half], u_pair[:half]), dot(w_row[h + 1, :half, :half], u_pair[:half])
            )
            near[half:, here] = jnp.where(
                lane < HEAD, dot(w_row[h, half:, :], u_pair), dot(w_row[h + 1, half:, :], u_pair)
            )

    def pass_on(g):
        part = pl.ds(g * group, group)
        send_col(i_send.at[:, :, part], got_i.at[:, :, part], i_out.at[g], i_in.at[g], across)

    def lined(v, g):
        return v[:, g * group : (g + 1) * group].reshape(lines, 1, group)

    def second(g):
        part = pl.ds(g * group, group)
        wait_for(got_l.at[:, :, part], l_in.at[g])

        @pl.when(place == 1)
        def _():
            joint = lined(own_decay, g) * got_l[:, :, part].astype(F32) + l_send[:, :, part].astype(F32)
            i_send[:, :, part] = joint.astype(BF16)
            pass_on(g)

    def finish(g, before_decay):
        part = pl.ds(g * group, group)
        wait_for(got_i.at[:, :, part], i_in.at[g])
        earlier = jnp.where(place == 1, 0.0, got_i[:, :, part].astype(F32))
        entering = lined(before_decay, g) * earlier + got_l[:, :, part].astype(F32)

        @pl.when(place == 2)
        def _():
            joint = lined(own_decay, g) * entering + l_send[:, :, part].astype(F32)
            i_send[:, :, part] = joint.astype(BF16)
            pass_on(g)

        carried = dot(c_lines, entering.reshape(lines * STATE, group).astype(BF16))
        y = near[:, part] + expand(from_start, spread[:, g * group : (g + 1) * group]) * carried
        y_send[:, :, :, part] = y.reshape(WINDOW, lines, 8, group).astype(BF16)
        for d in fro:
            send_col(
                y_send.at[middle + d, :, :, part], got_y.at[rows_of(me_col), :, part], y_out.at[g], y_in.at[g],
                around(me_col + d),
            )
        got_y[rows_of(me_col), :, part] = y_send[middle, :, :, part]

    for g in range(min(2, GROUPS)):
        enter(g)

    wait_for(got_f.at[pl.ds(0, tall - 1)], f_in.at[0])
    wait_for(got_t.at[pl.ds(0, tall - 1)], f_in.at[1])
    ends = jnp.concatenate([got_t[k, pl.ds(me_row, 1), :] for k in range(tall)], axis=0)
    decay = expand(jnp.exp2(ends[:, :HEADS]), spread, 3)
    carry = jnp.zeros((STATE, INNER), F32)
    for k in range(tall):
        s_send[k] = carry.astype(BF16)
        if k < tall - 1:
            carry = decay[k : k + 1] * carry + got_f[k].astype(F32)
    for q in row_peers:
        send_row(s_send.at[q], got_s.at[me_row], s_out, s_in, q)
    got_s[me_row] = s_send[me_row]

    def column_local():
        bar_col = jnp.where(same, 0.0, -1e30)
        scores_col = scores_of(c_col, b_col)
        run_col_t = transposed(run_col)
        skip_wide = expand(skip_ref[...], spread, 3)
        for pair in range(HEADS // 2):
            part = slice(pair * 128, pair * 128 + 128)
            top0, low0 = weights_of(run_col, run_col_t, scores_col, bar_col, 2 * pair)
            top1, low1 = weights_of(run_col, run_col_t, scores_col, bar_col, 2 * pair + 1)
            u = u_col[:, part]
            kept = skip_wide[:, part] * x_all[:, part]
            acc[:half, part] = jnp.where(lane < HEAD, dot(top0, u[:half]), dot(top1, u[:half])) + kept[:half]
            acc[half:, part] = jnp.where(lane < HEAD, dot(low0, u), dot(low1, u)) + kept[half:]

    for g in range(2, GROUPS):
        enter(g)
        if g == 2:
            column_local()
    if GROUPS <= 2:
        column_local()

    wait_for(got_e, e_in)
    before_decay = expand(got_e[:lines, :HEADS], spread, 3)
    second(0)
    for g in range(GROUPS):
        if g + 1 < GROUPS:
            second(g + 1)
        finish(g, before_decay)

    loads[4].wait()
    gate = gate_ref[...].astype(F32).reshape(tokens, INNER)
    act[...] = 0.5 * gate * (1.0 + jnp.tanh(0.5 * gate))

    wait_for(got_s.at[pl.ds(0, tall - 1)], s_in)
    entering_col = dot(c_wide, got_s[...].astype(F32).reshape(8 * STATE, INNER).astype(BF16))
    acc[...] += expand(jnp.exp2(run_col), spread) * entering_col

    power = jnp.zeros((tokens, 128), F32)
    for g in range(GROUPS):
        part = pl.ds(g * group, group)
        wait_for(got_y.at[pl.ds(0, (WINDOW - 1) * lines), :, part], y_in.at[g])
        y_row = got_y[:, :, part].astype(F32).reshape(tokens, group)
        v = (y_row + acc[:, part]) * act[:, part]
        mixed[:, part] = v
        for i in range(group // 128):
            w = v[:, i * 128 : i * 128 + 128]
            power += w * w
    scale = lax.rsqrt(jnp.sum(power, axis=1, keepdims=True) * (1.0 / INNER) + 1e-05)
    for i in range(INNER // 128):
        here = pl.ds(i * 128, 128)
        out_ref[:, :, here] = (mixed[:, here] * scale * gain_ref[i : i + 1, :]).reshape(tile_rows, 8, 128).astype(BF16)

    wait_near(got_bc, m_out.at[0])
    wait_near(got_dt, m_out.at[1])
    wait_for(f_send.at[pl.ds(0, tall - 1)], f_out.at[0])
    wait_for(got_t.at[pl.ds(0, tall - 1)], f_out.at[1])
    wait_for(s_send.at[pl.ds(0, tall - 1)], s_out)
    wait_for(e_send, e_out)
    for g in range(GROUPS):
        part = pl.ds(g * group, group)
        wait_near(got_x.at[:, :, :, part], x_out.at[g])
        wait_near(y_send.at[:, :, :, part], y_out.at[g])
        wait_for(l_send.at[:, :, part], l_out.at[g])
        wait_for(i_send.at[:, :, part], i_out.at[g])


def body(lanes, tall, x_in, gate_in, proj_bc, dt_raw, step_index, step_table, rates, skip, norm_gain):
    _, tile_rows, tile_cols, _ = x_in.shape
    tokens = tile_rows * tile_cols
    lines = tile_rows // WINDOW
    steps = step_table.shape[0]
    vmem = pl.BlockSpec(memory_space=pltpu.VMEM)
    smem = pl.BlockSpec(memory_space=pltpu.SMEM)
    hbm = pl.BlockSpec(memory_space=pl.ANY)
    dma = pltpu.SemaphoreType.DMA
    out = pl.pallas_call(
        functools.partial(kernel, lanes, tall),
        out_shape=jax.ShapeDtypeStruct((tile_rows, 8, INNER), BF16),
        in_specs=[smem, hbm, vmem, vmem, vmem, hbm, hbm, hbm, hbm],
        out_specs=vmem,
        scratch_shapes=[
            pltpu.VMEM((2 * HEADS, steps), F32),
            pltpu.VMEM((tile_rows, 8, INNER), BF16),
            pltpu.VMEM((tile_rows, 8, INNER), BF16),
            pltpu.VMEM((tile_rows, 8, 4 * STATE), BF16),
            pltpu.VMEM((tile_rows, 8, 2 * HEADS), BF16),
            dma((5,)),
            pltpu.VMEM((WINDOW, lines, 8, INNER), BF16),
            pltpu.VMEM((WINDOW, lines, 8, 4 * STATE), BF16),
            pltpu.VMEM((WINDOW, lines, 8, 2 * HEADS), BF16),
            pltpu.VMEM((WINDOW, lines, 8, INNER), BF16),
            pltpu.VMEM((tile_rows, 8, INNER), BF16),
            pltpu.VMEM((8, STATE, INNER), BF16),
            pltpu.VMEM((tall, STATE, INNER), BF16),
            pltpu.VMEM((8, 128), F32),
            pltpu.VMEM((tall, 8, 128), F32),
            pltpu.VMEM((tall, STATE, INNER), BF16),
            pltpu.VMEM((8, STATE, INNER), BF16),
            pltpu.VMEM((lines, STATE, INNER), BF16),
            pltpu.VMEM((lines, STATE, INNER), BF16),
            pltpu.VMEM((lines, STATE, INNER), BF16),
            pltpu.VMEM((lines, STATE, INNER), BF16),
            pltpu.VMEM((8, 128), F32),
            pltpu.VMEM((8, 128), F32),
            pltpu.VMEM((HEADS, tokens, tokens), BF16),
            pltpu.VMEM((tokens, INNER), F32),
            pltpu.VMEM((tokens, INNER), F32),
            pltpu.VMEM((tokens, INNER), F32),
            pltpu.VMEM((tokens, INNER), F32),
            pltpu.VMEM((tokens, INNER), F32),
            pltpu.VMEM((tokens, INNER), F32),
            dma((GROUPS,)),
            dma((GROUPS,)),
            dma((2,)),
            dma((2,)),
            dma((GROUPS,)),
            dma((GROUPS,)),
            dma((2,)),
            dma((2,)),
            dma,
            dma,
            dma((GROUPS,)),
            dma((GROUPS,)),
            dma((GROUPS,)),
            dma((GROUPS,)),
            dma,
            dma,
        ],
        compiler_params=pltpu.CompilerParams(
            collective_id=0, has_side_effects=True, vmem_limit_bytes=60 * 1024 * 1024
        ),
    )(
        step_index,
        step_table.T,
        rates,
        skip.reshape(1, HEADS),
        norm_gain.reshape(INNER // 128, 128),
        x_in.reshape(tile_rows, 8, INNER),
        gate_in.reshape(tile_rows, 8, INNER),
        proj_bc.reshape(tile_rows, 8, 4 * STATE),
        dt_raw.reshape(tile_rows, 8, 2 * HEADS),
    )
    return out.reshape(x_in.shape)


def solution(mesh):
    tile = P("img", "row", "col", None)
    return jax.shard_map(
        functools.partial(body, mesh.shape["col"], mesh.shape["row"]),
        mesh=mesh,
        in_specs=(tile, tile, tile, tile, P("img"), P(), P(), P(), P()),
        out_specs=tile,
        check_vma=False,
    )
```

```python
import functools

import jax
import jax.numpy as jnp
from jax import lax
from jax.experimental import pallas as pl
from jax.experimental.pallas import tpu as pltpu
from jax.sharding import PartitionSpec as P

HEADS = 24
HEAD = 64
STATE = 16
INNER = HEADS * HEAD
GROUPS = 4
WINDOW = 8
STAGES = 3
LOG2E = 1.4426950408889634
F32 = jnp.float32
BF16 = jnp.bfloat16


def dot(a, b):
    return jnp.dot(a, b, preferred_element_type=F32)


def split(v, pieces):
    parts = []
    for _ in range(pieces):
        part = v.astype(BF16)
        parts.append(part)
        v = v - part.astype(F32)
    return parts


def dot_exact(zero_one, v, pieces=3):
    return sum(dot(zero_one, part) for part in split(v, pieces))


def expand(v, heads_to_channels, pieces=2):
    return sum(dot(part, heads_to_channels) for part in split(v, pieces))


def softplus(v):
    return jnp.maximum(v, 0.0) + jnp.log(1.0 + jnp.exp(-jnp.abs(v)))


def kernel(
    lanes, tall, step_ref, table_hbm, rates_ref, skip_ref, gain_ref, x_hbm, gate_hbm, bc_hbm, dt_hbm, out_ref,
    table_ref, x_ref, gate_ref, bc_ref, dt_ref, load_sem,
    got_x, got_bc, got_dt, y_send, got_y, f_send, got_f, t_send, got_t, s_send, got_s,
    l_send, got_l, i_send, got_i, e_send, got_e, w_row, u_row_s, end_s, near, acc, act, mixed,
    x_out, x_in, m_out, m_in, y_out, y_in, f_out, f_in, s_out, s_in, l_out, l_in, i_out, i_in, e_out, e_in, known,
):
    tile_rows = x_ref.shape[0]
    tokens = tile_rows * 8
    half = tokens // 2
    windows = lanes // WINDOW
    lines = tile_rows // WINDOW
    group = INNER // GROUPS
    group_heads = HEADS // GROUPS
    middle = WINDOW // 2
    me_col = lax.axis_index("col")
    me_row = lax.axis_index("row")

    def around(c):
        return (c + 2 * lanes) % lanes

    def rows_of(c):
        return pl.ds(((c + middle) % WINDOW) * lines, lines)

    order = sorted(range(1, middle + 1), reverse=True)
    to = [d for k in order for d in ((k, -k) if k < middle else (k,))]
    fro = [d for k in order for d in ((-k, k) if k < middle else (-k,))]
    row_peers = [(me_row + k) % tall for k in range(1, tall)]
    after, before, across = around(me_col + WINDOW), around(me_col - WINDOW), around(me_col + 2 * WINDOW)
    place = ((me_col + middle - 1) % lanes) // WINDOW
    cut = around(middle - me_col)
    cut_in = jnp.where(place == 0, cut, WINDOW)
    cut_out = jnp.where(place == 0, cut, 0)

    barrier = pltpu.get_barrier_semaphore()

    def greet(**device):
        pl.semaphore_signal(barrier, inc=1, device_id=device, device_id_type=pl.DeviceIdType.MESH)

    greeted = [around(me_col + 1), around(me_col - 1)] + ([across] if windows > 2 else [])
    for c in greeted:
        greet(col=c)
    for q in row_peers:
        greet(row=q)

    loads = []
    for i, (src, dst) in enumerate(
        ((bc_hbm, bc_ref), (dt_hbm, dt_ref), (table_hbm, table_ref), (x_hbm, x_ref), (gate_hbm, gate_ref))
    ):
        loads.append(pltpu.make_async_copy(src, dst, load_sem.at[i]))
        loads[-1].start()

    def send_col(src, dst, out_sem, in_sem, p):
        pltpu.make_async_remote_copy(
            src_ref=src, dst_ref=dst, send_sem=out_sem, recv_sem=in_sem,
            device_id={"col": p}, device_id_type=pl.DeviceIdType.MESH,
        ).start()

    def send_row(src, dst, out_sem, in_sem, q):
        pltpu.make_async_remote_copy(
            src_ref=src, dst_ref=dst, send_sem=out_sem, recv_sem=in_sem,
            device_id={"row": q}, device_id_type=pl.DeviceIdType.MESH,
        ).start()

    def wait_for(ref, sem):
        pltpu.make_async_copy(ref, ref, sem).wait()

    rows = lax.broadcasted_iota(jnp.int32, (tokens, tokens), 0)
    cols = lax.broadcasted_iota(jnp.int32, (tokens, tokens), 1)
    causal = rows >= cols
    same = causal & ((rows & 7) == (cols & 7))
    channel = lax.broadcasted_iota(jnp.int32, (HEADS, INNER), 1)
    head = lax.broadcasted_iota(jnp.int32, (HEADS, INNER), 0)
    spread = ((channel >= head * HEAD) & (channel < (head + 1) * HEAD)).astype(BF16)

    def widen(v, kept, count):
        wide = count * STATE
        fan = (
            (lax.broadcasted_iota(jnp.int32, (STATE, wide), 1) & (STATE - 1))
            == lax.broadcasted_iota(jnp.int32, (STATE, wide), 0)
        ).astype(BF16)
        return jnp.where(kept, dot(v, fan), 0.0)

    for i in range(4):
        loads[i].wait()
    chosen = (lax.broadcasted_iota(jnp.int32, (8, table_ref.shape[1]), 1) == step_ref[0]).astype(BF16)
    bias = sum(
        lax.dot_general(chosen, part, (((1,), (1,)), ((), ())), preferred_element_type=F32)
        for part in split(table_ref[...], 3)
    )[0:1]
    dt_own = dt_ref[...].astype(F32).reshape(tokens, 2 * HEADS)
    dt_col = softplus(dt_own[:, HEADS:] + bias[:, HEADS:])
    log_col = dt_col * (-LOG2E * rates_ref[1:2, :])
    run_col = dot_exact(same.astype(BF16), log_col)
    run3 = run_col.reshape(tile_rows, 8, HEADS)
    end_col = run3[tile_rows - 1]
    to_end = jnp.exp2(end_col[None] - run3).reshape(tokens, HEADS)
    x_all = x_ref[...].astype(F32).reshape(tokens, INNER)
    u_col = (expand(dt_col, spread) * x_all).astype(BF16)
    bc_own = bc_ref[...].astype(F32).reshape(tokens, 4 * STATE)
    b_col = bc_own[:, 2 * STATE : 3 * STATE].astype(BF16)
    c_col = bc_own[:, 3 * STATE :].astype(BF16)
    own_col = (lax.broadcasted_iota(jnp.int32, (tokens, 8 * STATE), 1) // STATE) == (
        lax.broadcasted_iota(jnp.int32, (tokens, 8 * STATE), 0) & 7
    )
    c_wide = widen(c_col, own_col, 8).astype(BF16)
    u_end = (expand(to_end, spread) * u_col.astype(F32)).astype(BF16)
    states = dot(widen(b_col, own_col, 8).T.astype(BF16), u_end)
    f_send[...] = states.astype(BF16).reshape(8, STATE, INNER)
    t_send[...] = jnp.concatenate([end_col, jnp.zeros((8, 128 - HEADS), F32)], axis=1)

    def send_states():
        for q in row_peers:
            send_row(f_send.at[q], got_f.at[me_row], f_out.at[0], f_in.at[0], q)
            send_row(t_send, got_t.at[me_row], f_out.at[1], f_in.at[1], q)

    def send_small(stage, d):
        c = around(me_col + d)
        send_col(bc_ref.at[rows_of(c)], got_bc.at[middle - d], m_out.at[0], m_in.at[2 * stage], c)
        send_col(dt_ref.at[rows_of(c)], got_dt.at[middle - d], m_out.at[1], m_in.at[2 * stage + 1], c)

    def send_tokens(g, chosen):
        part = pl.ds(g * group, group)
        for d in chosen:
            c = around(me_col + d)
            send_col(x_ref.at[rows_of(c), :, part], got_x.at[middle - d, :, :, part], x_out.at[g], x_in.at[g], c)

    pl.semaphore_wait(barrier, len(greeted) + tall - 1)

    reach = [0] + [1 << i for i in range(STAGES - 1)] + [middle]
    for stage in range(STAGES):
        if stage:
            count = sum(reach[stage - 1] < abs(d) <= reach[stage] for d in fro)
            wait_for(got_bc.at[pl.ds(0, count)], m_in.at[2 * stage - 2])
            wait_for(got_dt.at[pl.ds(0, count)], m_in.at[2 * stage - 1])
        chosen_to = [d for d in to if reach[stage] < abs(d) <= reach[stage + 1]]
        for d in chosen_to:
            send_small(stage, d)
        for g in range(GROUPS):
            send_tokens(g, chosen_to)
        if stage == 0:
            send_states()
    pl.semaphore_signal(known, inc=1, device_id={"col": around(me_col - middle)}, device_id_type=pl.DeviceIdType.MESH)
    got_bc[middle] = bc_ref[rows_of(me_col)]
    got_dt[middle] = dt_ref[rows_of(me_col)]
    got_x[middle] = x_ref[rows_of(me_col)]
    got_f[me_row] = f_send[me_row]
    got_t[me_row] = t_send[...]

    def wait_near(ref, sem):
        wait_for(ref.at[pl.ds(0, WINDOW - 1)], sem)

    def weights_of(run, run_t, scores, bar, h):
        top = jnp.exp2(run[:half, h : h + 1] - run_t[h : h + 1, :half] + bar[:half, :half]) * scores[:half, :half]
        low = jnp.exp2(run[half:, h : h + 1] - run_t[h : h + 1, :] + bar[half:, :]) * scores[half:, :]
        return top.astype(BF16), low.astype(BF16)

    def transposed(run):
        return jnp.concatenate([run, jnp.zeros((tokens, 128 - HEADS), F32)], axis=1).T

    def scores_of(c, b):
        return lax.dot_general(c, b, (((1,), (1,)), ((), ())), preferred_element_type=F32)

    lane = lax.broadcasted_iota(jnp.int32, (1, 128), 1)

    last = sum(abs(d) > reach[STAGES - 1] for d in fro)
    wait_for(got_bc.at[pl.ds(0, last)], m_in.at[2 * STAGES - 2])
    wait_for(got_dt.at[pl.ds(0, last)], m_in.at[2 * STAGES - 1])
    pl.semaphore_wait(known, 1)
    line_size = 8 * lines
    tile_i, tile_j = rows // line_size, cols // line_size
    line_i, line_j = (rows // 8) % lines, (cols // 8) % lines
    joined = causal & (line_i == line_j) & ((tile_i >= cut_out) == (tile_j >= cut_out))
    bc_line = got_bc[...].astype(F32).reshape(tokens, 4 * STATE)
    dt_line = got_dt[...].astype(F32).reshape(tokens, 2 * HEADS)
    dt_row = softplus(dt_line[:, :HEADS] + bias[:, :HEADS])
    log_row = dt_row * (-LOG2E * rates_ref[0:1, :])
    run_row = dot_exact(joined.astype(BF16), log_row)
    ends_row = run_row.reshape(WINDOW, lines, 8, HEADS)[WINDOW - 1, :, 7:8, :]
    run4 = run_row.reshape(WINDOW, lines, 8, HEADS)
    tile4 = lax.broadcasted_iota(jnp.int32, (WINDOW, lines, 8, HEADS), 0)
    to_end_row = jnp.where(tile4 >= cut_out, jnp.exp2(ends_row[None] - run4), 0.0).reshape(tokens, HEADS)
    from_start = jnp.where(tile4 < cut_in, jnp.exp2(run4), 0.0).reshape(tokens, HEADS)
    own_line = (lax.broadcasted_iota(jnp.int32, (tokens, lines * STATE), 1) // STATE) == (
        lax.broadcasted_iota(jnp.int32, (tokens, lines * STATE), 0) // 8
    ) % lines
    b_row = bc_line[:, :STATE].astype(BF16)
    c_row = bc_line[:, STATE : 2 * STATE].astype(BF16)
    b_lines = widen(b_row, own_line, lines).T.astype(BF16)
    c_lines = widen(c_row, own_line, lines).astype(BF16)
    u_row_s[...] = expand(dt_row, spread)
    end_s[...] = expand(to_end_row, spread)
    line_decay = jnp.exp2(ends_row.reshape(lines, HEADS))
    e_send[...] = jnp.concatenate(
        [
            jnp.concatenate([line_decay, jnp.zeros((8 - lines, HEADS), F32)], axis=0),
            jnp.zeros((8, 128 - HEADS), F32),
        ],
        axis=1,
    )
    own_decay = expand(line_decay, spread, 3)
    send_col(e_send, got_e, e_out, e_in, after)
    scores_row = scores_of(c_row, b_row)
    run_row_t = transposed(run_row)
    bar_row = jnp.where(joined, 0.0, -1e30)
    for h in range(HEADS):
        top, low = weights_of(run_row, run_row_t, scores_row, bar_row, h)
        w_row[h, :half, :half] = top
        w_row[h, half:, :] = low

    def enter(g):
        part = pl.ds(g * group, group)
        wait_near(got_x.at[:, :, :, part], x_in.at[g])
        x_line = got_x[:, :, :, part].astype(F32).reshape(tokens, group)
        u = (u_row_s[:, part] * x_line).astype(BF16)
        u_end = (end_s[:, part] * u.astype(F32)).astype(BF16)
        state = dot(b_lines, u_end)
        l_send[:, :, part] = state.reshape(lines, STATE, group).astype(BF16)
        send_col(l_send.at[:, :, part], got_l.at[:, :, part], l_out.at[g], l_in.at[g], after)

        @pl.when((place == 0) | (place == windows - 1))
        def _():
            i_send[:, :, part] = state.reshape(lines, STATE, group).astype(BF16)
            pass_on(g)

        for i in range(group_heads // 2):
            h = g * group_heads + 2 * i
            u_pair = u[:, i * 128 : i * 128 + 128]
            here = pl.ds(h * HEAD, 128)
            near[:half, here] = jnp.where(
                lane < HEAD, dot(w_row[h, :half, :half], u_pair[:half]), dot(w_row[h + 1, :half, :half], u_pair[:half])
            )
            near[half:, here] = jnp.where(
                lane < HEAD, dot(w_row[h, half:, :], u_pair), dot(w_row[h + 1, half:, :], u_pair)
            )

    def pass_on(g):
        part = pl.ds(g * group, group)
        send_col(i_send.at[:, :, part], got_i.at[:, :, part], i_out.at[g], i_in.at[g], across)

    def lined(v, g):
        return v[:, g * group : (g + 1) * group].reshape(lines, 1, group)

    def second(g):
        part = pl.ds(g * group, group)
        wait_for(got_l.at[:, :, part], l_in.at[g])

        @pl.when(place == 1)
        def _():
            joint = lined(own_decay, g) * got_l[:, :, part].astype(F32) + l_send[:, :, part].astype(F32)
            i_send[:, :, part] = joint.astype(BF16)
            pass_on(g)

    def finish(g, before_decay):
        part = pl.ds(g * group, group)
        wait_for(got_i.at[:, :, part], i_in.at[g])
        earlier = jnp.where(place == 1, 0.0, got_i[:, :, part].astype(F32))
        entering = lined(before_decay, g) * earlier + got_l[:, :, part].astype(F32)

        @pl.when(place == 2)
        def _():
            joint = lined(own_decay, g) * entering + l_send[:, :, part].astype(F32)
            i_send[:, :, part] = joint.astype(BF16)
            pass_on(g)

        carried = dot(c_lines, entering.reshape(lines * STATE, group).astype(BF16))
        y = near[:, part] + expand(from_start, spread[:, g * group : (g + 1) * group]) * carried
        y_send[:, :, :, part] = y.reshape(WINDOW, lines, 8, group).astype(BF16)
        for d in fro:
            send_col(
                y_send.at[middle + d, :, :, part], got_y.at[rows_of(me_col), :, part], y_out.at[g], y_in.at[g],
                around(me_col + d),
            )
        got_y[rows_of(me_col), :, part] = y_send[middle, :, :, part]

    for g in range(min(2, GROUPS)):
        enter(g)

    wait_for(got_f.at[pl.ds(0, tall - 1)], f_in.at[0])
    wait_for(got_t.at[pl.ds(0, tall - 1)], f_in.at[1])
    ends = jnp.concatenate([got_t[k, pl.ds(me_row, 1), :] for k in range(tall)], axis=0)
    decay = expand(jnp.exp2(ends[:, :HEADS]), spread, 3)
    carry = jnp.zeros((STATE, INNER), F32)
    for k in range(tall):
        s_send[k] = carry.astype(BF16)
        if k < tall - 1:
            carry = decay[k : k + 1] * carry + got_f[k].astype(F32)
    for q in row_peers:
        send_row(s_send.at[q], got_s.at[me_row], s_out, s_in, q)
    got_s[me_row] = s_send[me_row]

    def column_local():
        bar_col = jnp.where(same, 0.0, -1e30)
        scores_col = scores_of(c_col, b_col)
        run_col_t = transposed(run_col)
        skip_wide = expand(skip_ref[...], spread, 3)
        for pair in range(HEADS // 2):
            part = slice(pair * 128, pair * 128 + 128)
            top0, low0 = weights_of(run_col, run_col_t, scores_col, bar_col, 2 * pair)
            top1, low1 = weights_of(run_col, run_col_t, scores_col, bar_col, 2 * pair + 1)
            u = u_col[:, part]
            kept = skip_wide[:, part] * x_all[:, part]
            acc[:half, part] = jnp.where(lane < HEAD, dot(top0, u[:half]), dot(top1, u[:half])) + kept[:half]
            acc[half:, part] = jnp.where(lane < HEAD, dot(low0, u), dot(low1, u)) + kept[half:]

    for g in range(2, GROUPS):
        enter(g)
        if g == 2:
            column_local()
    if GROUPS <= 2:
        column_local()

    wait_for(got_e, e_in)
    before_decay = expand(got_e[:lines, :HEADS], spread, 3)
    second(0)
    for g in range(GROUPS):
        if g + 1 < GROUPS:
            second(g + 1)
        finish(g, before_decay)

    loads[4].wait()
    gate = gate_ref[...].astype(F32).reshape(tokens, INNER)
    act[...] = 0.5 * gate * (1.0 + jnp.tanh(0.5 * gate))

    wait_for(got_s.at[pl.ds(0, tall - 1)], s_in)
    entering_col = dot(c_wide, got_s[...].astype(F32).reshape(8 * STATE, INNER).astype(BF16))
    acc[...] += expand(jnp.exp2(run_col), spread) * entering_col

    power = jnp.zeros((tokens, 128), F32)
    for g in range(GROUPS):
        part = pl.ds(g * group, group)
        wait_for(got_y.at[pl.ds(0, (WINDOW - 1) * lines), :, part], y_in.at[g])
        y_row = got_y[:, :, part].astype(F32).reshape(tokens, group)
        v = (y_row + acc[:, part]) * act[:, part]
        mixed[:, part] = v
        for i in range(group // 128):
            w = v[:, i * 128 : i * 128 + 128]
            power += w * w
    scale = lax.rsqrt(jnp.sum(power, axis=1, keepdims=True) * (1.0 / INNER) + 1e-05)
    for i in range(INNER // 128):
        here = pl.ds(i * 128, 128)
        out_ref[:, :, here] = (mixed[:, here] * scale * gain_ref[i : i + 1, :]).reshape(tile_rows, 8, 128).astype(BF16)

    wait_near(got_bc, m_out.at[0])
    wait_near(got_dt, m_out.at[1])
    wait_for(f_send.at[pl.ds(0, tall - 1)], f_out.at[0])
    wait_for(got_t.at[pl.ds(0, tall - 1)], f_out.at[1])
    wait_for(s_send.at[pl.ds(0, tall - 1)], s_out)
    wait_for(e_send, e_out)
    for g in range(GROUPS):
        part = pl.ds(g * group, group)
        wait_near(got_x.at[:, :, :, part], x_out.at[g])
        wait_near(y_send.at[:, :, :, part], y_out.at[g])
        wait_for(l_send.at[:, :, part], l_out.at[g])
        wait_for(i_send.at[:, :, part], i_out.at[g])


def body(lanes, tall, x_in, gate_in, proj_bc, dt_raw, step_index, step_table, rates, skip, norm_gain):
    _, tile_rows, tile_cols, _ = x_in.shape
    tokens = tile_rows * tile_cols
    lines = tile_rows // WINDOW
    steps = step_table.shape[0]
    vmem = pl.BlockSpec(memory_space=pltpu.VMEM)
    smem = pl.BlockSpec(memory_space=pltpu.SMEM)
    hbm = pl.BlockSpec(memory_space=pl.ANY)
    dma = pltpu.SemaphoreType.DMA
    out = pl.pallas_call(
        functools.partial(kernel, lanes, tall),
        out_shape=jax.ShapeDtypeStruct((tile_rows, 8, INNER), BF16),
        in_specs=[smem, hbm, vmem, vmem, vmem, hbm, hbm, hbm, hbm],
        out_specs=vmem,
        scratch_shapes=[
            pltpu.VMEM((2 * HEADS, steps), F32),
            pltpu.VMEM((tile_rows, 8, INNER), BF16),
            pltpu.VMEM((tile_rows, 8, INNER), BF16),
            pltpu.VMEM((tile_rows, 8, 4 * STATE), BF16),
            pltpu.VMEM((tile_rows, 8, 2 * HEADS), BF16),
            dma((5,)),
            pltpu.VMEM((WINDOW, lines, 8, INNER), BF16),
            pltpu.VMEM((WINDOW, lines, 8, 4 * STATE), BF16),
            pltpu.VMEM((WINDOW, lines, 8, 2 * HEADS), BF16),
            pltpu.VMEM((WINDOW, lines, 8, INNER), BF16),
            pltpu.VMEM((tile_rows, 8, INNER), BF16),
            pltpu.VMEM((8, STATE, INNER), BF16),
            pltpu.VMEM((tall, STATE, INNER), BF16),
            pltpu.VMEM((8, 128), F32),
            pltpu.VMEM((tall, 8, 128), F32),
            pltpu.VMEM((tall, STATE, INNER), BF16),
            pltpu.VMEM((8, STATE, INNER), BF16),
            pltpu.VMEM((lines, STATE, INNER), BF16),
            pltpu.VMEM((lines, STATE, INNER), BF16),
            pltpu.VMEM((lines, STATE, INNER), BF16),
            pltpu.VMEM((lines, STATE, INNER), BF16),
            pltpu.VMEM((8, 128), F32),
            pltpu.VMEM((8, 128), F32),
            pltpu.VMEM((HEADS, tokens, tokens), BF16),
            pltpu.VMEM((tokens, INNER), F32),
            pltpu.VMEM((tokens, INNER), F32),
            pltpu.VMEM((tokens, INNER), F32),
            pltpu.VMEM((tokens, INNER), F32),
            pltpu.VMEM((tokens, INNER), F32),
            pltpu.VMEM((tokens, INNER), F32),
            dma((GROUPS,)),
            dma((GROUPS,)),
            dma((2,)),
            dma((2 * STAGES,)),
            dma((GROUPS,)),
            dma((GROUPS,)),
            dma((2,)),
            dma((2,)),
            dma,
            dma,
            dma((GROUPS,)),
            dma((GROUPS,)),
            dma((GROUPS,)),
            dma((GROUPS,)),
            dma,
            dma,
            pltpu.SemaphoreType.REGULAR,
        ],
        compiler_params=pltpu.CompilerParams(
            collective_id=0, has_side_effects=True, vmem_limit_bytes=60 * 1024 * 1024
        ),
    )(
        step_index,
        step_table.T,
        rates,
        skip.reshape(1, HEADS),
        norm_gain.reshape(INNER // 128, 128),
        x_in.reshape(tile_rows, 8, INNER),
        gate_in.reshape(tile_rows, 8, INNER),
        proj_bc.reshape(tile_rows, 8, 4 * STATE),
        dt_raw.reshape(tile_rows, 8, 2 * HEADS),
    )
    return out.reshape(x_in.shape)


def solution(mesh):
    tile = P("img", "row", "col", None)
    return jax.shard_map(
        functools.partial(body, mesh.shape["col"], mesh.shape["row"]),
        mesh=mesh,
        in_specs=(tile, tile, tile, tile, P("img"), P(), P(), P(), P()),
        out_specs=tile,
        check_vma=False,
    )
```

```python
import functools

import jax
import jax.numpy as jnp
from jax import lax
from jax.experimental import pallas as pl
from jax.experimental.pallas import tpu as pltpu
from jax.sharding import PartitionSpec as P

HEADS = 24
HEAD = 64
STATE = 16
INNER = HEADS * HEAD
GROUPS = 4
WINDOW = 8
LOG2E = 1.4426950408889634
F32 = jnp.float32
BF16 = jnp.bfloat16


def dot(a, b):
    return jnp.dot(a, b, preferred_element_type=F32)


def split(v, pieces):
    parts = []
    for _ in range(pieces):
        part = v.astype(BF16)
        parts.append(part)
        v = v - part.astype(F32)
    return parts


def dot_exact(zero_one, v, pieces=3):
    return sum(dot(zero_one, part) for part in split(v, pieces))


def expand(v, heads_to_channels, pieces=2):
    return sum(dot(part, heads_to_channels) for part in split(v, pieces))


def softplus(v):
    return jnp.maximum(v, 0.0) + jnp.log(1.0 + jnp.exp(-jnp.abs(v)))


def kernel(
    lanes, tall, step_ref, table_hbm, rates_ref, skip_ref, gain_ref, x_hbm, gate_hbm, bc_hbm, dt_hbm, out_ref,
    table_ref, x_ref, gate_ref, bc_ref, dt_ref, load_sem,
    got_x, got_bc, got_dt, y_send, got_y, f_send, got_f, t_send, got_t, s_send, got_s,
    l_send, got_l, i_send, got_i, e_send, got_e, w_row, u_row_s, end_s, near, acc, act, mixed,
    x_out, x_in, m_out, m_in, y_out, y_in, f_out, f_in, s_out, s_in, l_out, l_in, i_out, i_in, e_out, e_in, known,
):
    tile_rows = x_ref.shape[0]
    tokens = tile_rows * 8
    half = tokens // 2
    windows = lanes // WINDOW
    lines = tile_rows // WINDOW
    group = INNER // GROUPS
    group_heads = HEADS // GROUPS
    middle = WINDOW // 2
    me_col = lax.axis_index("col")
    me_row = lax.axis_index("row")

    def around(c):
        return (c + 2 * lanes) % lanes

    def rows_of(c):
        return pl.ds(((c + middle) % WINDOW) * lines, lines)

    order = sorted(range(1, middle + 1), reverse=True)
    to = [d for k in order for d in ((k, -k) if k < middle else (k,))]
    fro = [d for k in order for d in ((-k, k) if k < middle else (-k,))]
    row_peers = [(me_row + k) % tall for k in range(1, tall)]
    after, before, across = around(me_col + WINDOW), around(me_col - WINDOW), around(me_col + 2 * WINDOW)
    place = ((me_col + middle - 1) % lanes) // WINDOW
    cut = around(middle - me_col)
    cut_in = jnp.where(place == 0, cut, WINDOW)
    cut_out = jnp.where(place == 0, cut, 0)

    barrier = pltpu.get_barrier_semaphore()

    def greet(**device):
        pl.semaphore_signal(barrier, inc=1, device_id=device, device_id_type=pl.DeviceIdType.MESH)

    near_set = sorted(set(to) | set(fro))
    greeted = [around(me_col + d) for d in near_set] + ([across] if windows > 2 else [])
    for c in greeted:
        greet(col=c)
    for q in row_peers:
        greet(row=q)

    loads = []
    for i, (src, dst) in enumerate(
        ((bc_hbm, bc_ref), (dt_hbm, dt_ref), (table_hbm, table_ref), (x_hbm, x_ref), (gate_hbm, gate_ref))
    ):
        loads.append(pltpu.make_async_copy(src, dst, load_sem.at[i]))
        loads[-1].start()

    def send_col(src, dst, out_sem, in_sem, p):
        pltpu.make_async_remote_copy(
            src_ref=src, dst_ref=dst, send_sem=out_sem, recv_sem=in_sem,
            device_id={"col": p}, device_id_type=pl.DeviceIdType.MESH,
        ).start()

    def send_row(src, dst, out_sem, in_sem, q):
        pltpu.make_async_remote_copy(
            src_ref=src, dst_ref=dst, send_sem=out_sem, recv_sem=in_sem,
            device_id={"row": q}, device_id_type=pl.DeviceIdType.MESH,
        ).start()

    def wait_for(ref, sem):
        pltpu.make_async_copy(ref, ref, sem).wait()

    rows = lax.broadcasted_iota(jnp.int32, (tokens, tokens), 0)
    cols = lax.broadcasted_iota(jnp.int32, (tokens, tokens), 1)
    causal = rows >= cols
    same = causal & ((rows & 7) == (cols & 7))
    channel = lax.broadcasted_iota(jnp.int32, (HEADS, INNER), 1)
    head = lax.broadcasted_iota(jnp.int32, (HEADS, INNER), 0)
    spread = ((channel >= head * HEAD) & (channel < (head + 1) * HEAD)).astype(BF16)

    def widen(v, kept, count):
        wide = count * STATE
        fan = (
            (lax.broadcasted_iota(jnp.int32, (STATE, wide), 1) & (STATE - 1))
            == lax.broadcasted_iota(jnp.int32, (STATE, wide), 0)
        ).astype(BF16)
        return jnp.where(kept, dot(v, fan), 0.0)

    for i in range(4):
        loads[i].wait()
    chosen = (lax.broadcasted_iota(jnp.int32, (8, table_ref.shape[1]), 1) == step_ref[0]).astype(BF16)
    bias = sum(
        lax.dot_general(chosen, part, (((1,), (1,)), ((), ())), preferred_element_type=F32)
        for part in split(table_ref[...], 3)
    )[0:1]
    dt_own = dt_ref[...].astype(F32).reshape(tokens, 2 * HEADS)
    dt_col = softplus(dt_own[:, HEADS:] + bias[:, HEADS:])
    log_col = dt_col * (-LOG2E * rates_ref[1:2, :])
    run_col = dot_exact(same.astype(BF16), log_col)
    run3 = run_col.reshape(tile_rows, 8, HEADS)
    end_col = run3[tile_rows - 1]
    to_end = jnp.exp2(end_col[None] - run3).reshape(tokens, HEADS)
    x_all = x_ref[...].astype(F32).reshape(tokens, INNER)
    u_col = (expand(dt_col, spread) * x_all).astype(BF16)
    bc_own = bc_ref[...].astype(F32).reshape(tokens, 4 * STATE)
    b_col = bc_own[:, 2 * STATE : 3 * STATE].astype(BF16)
    c_col = bc_own[:, 3 * STATE :].astype(BF16)
    own_col = (lax.broadcasted_iota(jnp.int32, (tokens, 8 * STATE), 1) // STATE) == (
        lax.broadcasted_iota(jnp.int32, (tokens, 8 * STATE), 0) & 7
    )
    c_wide = widen(c_col, own_col, 8).astype(BF16)
    u_end = (expand(to_end, spread) * u_col.astype(F32)).astype(BF16)
    states = dot(widen(b_col, own_col, 8).T.astype(BF16), u_end)
    f_send[...] = states.astype(BF16).reshape(8, STATE, INNER)
    t_send[...] = jnp.concatenate([end_col, jnp.zeros((8, 128 - HEADS), F32)], axis=1)

    def send_states():
        for q in row_peers:
            send_row(f_send.at[q], got_f.at[me_row], f_out.at[0], f_in.at[0], q)
            send_row(t_send, got_t.at[me_row], f_out.at[1], f_in.at[1], q)

    def send_small(d):
        c = around(me_col + d)
        send_col(bc_ref.at[rows_of(c)], got_bc.at[middle - d], m_out.at[0], m_in.at[0], c)
        send_col(dt_ref.at[rows_of(c)], got_dt.at[middle - d], m_out.at[1], m_in.at[1], c)

    def send_tokens(g):
        part = pl.ds(g * group, group)
        for d in to:
            c = around(me_col + d)
            send_col(x_ref.at[rows_of(c), :, part], got_x.at[middle - d, :, :, part], x_out.at[g], x_in.at[g], c)

    pl.semaphore_wait(barrier, len(greeted) + tall - 1)

    for d in to:
        send_small(d)
    send_states()
    for g in range(GROUPS):
        send_tokens(g)
    pl.semaphore_signal(known, inc=1, device_id={"col": around(me_col - middle)}, device_id_type=pl.DeviceIdType.MESH)
    got_bc[middle] = bc_ref[rows_of(me_col)]
    got_dt[middle] = dt_ref[rows_of(me_col)]
    got_x[middle] = x_ref[rows_of(me_col)]
    got_f[me_row] = f_send[me_row]
    got_t[me_row] = t_send[...]

    def wait_near(ref, sem):
        wait_for(ref.at[pl.ds(0, WINDOW - 1)], sem)

    def weights_of(run, run_t, scores, bar, h):
        top = jnp.exp2(run[:half, h : h + 1] - run_t[h : h + 1, :half] + bar[:half, :half]) * scores[:half, :half]
        low = jnp.exp2(run[half:, h : h + 1] - run_t[h : h + 1, :] + bar[half:, :]) * scores[half:, :]
        return top.astype(BF16), low.astype(BF16)

    def transposed(run):
        return jnp.concatenate([run, jnp.zeros((tokens, 128 - HEADS), F32)], axis=1).T

    def scores_of(c, b):
        return lax.dot_general(c, b, (((1,), (1,)), ((), ())), preferred_element_type=F32)

    lane = lax.broadcasted_iota(jnp.int32, (1, 128), 1)

    wait_near(got_bc, m_in.at[0])
    wait_near(got_dt, m_in.at[1])
    pl.semaphore_wait(known, 1)
    line_size = 8 * lines
    tile_i, tile_j = rows // line_size, cols // line_size
    line_i, line_j = (rows // 8) % lines, (cols // 8) % lines
    joined = causal & (line_i == line_j) & ((tile_i >= cut_out) == (tile_j >= cut_out))
    bc_line = got_bc[...].astype(F32).reshape(tokens, 4 * STATE)
    dt_line = got_dt[...].astype(F32).reshape(tokens, 2 * HEADS)
    dt_row = softplus(dt_line[:, :HEADS] + bias[:, :HEADS])
    log_row = dt_row * (-LOG2E * rates_ref[0:1, :])
    run_row = dot_exact(joined.astype(BF16), log_row)
    ends_row = run_row.reshape(WINDOW, lines, 8, HEADS)[WINDOW - 1, :, 7:8, :]
    run4 = run_row.reshape(WINDOW, lines, 8, HEADS)
    tile4 = lax.broadcasted_iota(jnp.int32, (WINDOW, lines, 8, HEADS), 0)
    to_end_row = jnp.where(tile4 >= cut_out, jnp.exp2(ends_row[None] - run4), 0.0).reshape(tokens, HEADS)
    from_start = jnp.where(tile4 < cut_in, jnp.exp2(run4), 0.0).reshape(tokens, HEADS)
    own_line = (lax.broadcasted_iota(jnp.int32, (tokens, lines * STATE), 1) // STATE) == (
        lax.broadcasted_iota(jnp.int32, (tokens, lines * STATE), 0) // 8
    ) % lines
    b_row = bc_line[:, :STATE].astype(BF16)
    c_row = bc_line[:, STATE : 2 * STATE].astype(BF16)
    b_lines = widen(b_row, own_line, lines).T.astype(BF16)
    c_lines = widen(c_row, own_line, lines).astype(BF16)
    u_row_s[...] = expand(dt_row, spread)
    end_s[...] = expand(to_end_row, spread)
    line_decay = jnp.exp2(ends_row.reshape(lines, HEADS))
    e_send[...] = jnp.concatenate(
        [
            jnp.concatenate([line_decay, jnp.zeros((8 - lines, HEADS), F32)], axis=0),
            jnp.zeros((8, 128 - HEADS), F32),
        ],
        axis=1,
    )
    own_decay = expand(line_decay, spread, 3)
    send_col(e_send, got_e, e_out, e_in, after)
    scores_row = scores_of(c_row, b_row)
    run_row_t = transposed(run_row)
    bar_row = jnp.where(joined, 0.0, -1e30)
    for h in range(HEADS):
        top, low = weights_of(run_row, run_row_t, scores_row, bar_row, h)
        w_row[h, :half, :half] = top
        w_row[h, half:, :] = low

    def enter(g):
        part = pl.ds(g * group, group)
        wait_near(got_x.at[:, :, :, part], x_in.at[g])
        x_line = got_x[:, :, :, part].astype(F32).reshape(tokens, group)
        u = (u_row_s[:, part] * x_line).astype(BF16)
        u_end = (end_s[:, part] * u.astype(F32)).astype(BF16)
        state = dot(b_lines, u_end)
        l_send[:, :, part] = state.reshape(lines, STATE, group).astype(BF16)
        send_col(l_send.at[:, :, part], got_l.at[:, :, part], l_out.at[g], l_in.at[g], after)

        @pl.when((place == 0) | (place == windows - 1))
        def _():
            i_send[:, :, part] = state.reshape(lines, STATE, group).astype(BF16)
            pass_on(g)

        for i in range(group_heads // 2):
            h = g * group_heads + 2 * i
            u_pair = u[:, i * 128 : i * 128 + 128]
            here = pl.ds(h * HEAD, 128)
            near[:half, here] = jnp.where(
                lane < HEAD, dot(w_row[h, :half, :half], u_pair[:half]), dot(w_row[h + 1, :half, :half], u_pair[:half])
            )
            near[half:, here] = jnp.where(
                lane < HEAD, dot(w_row[h, half:, :], u_pair), dot(w_row[h + 1, half:, :], u_pair)
            )

    def pass_on(g):
        part = pl.ds(g * group, group)
        send_col(i_send.at[:, :, part], got_i.at[:, :, part], i_out.at[g], i_in.at[g], across)

    def lined(v, g):
        return v[:, g * group : (g + 1) * group].reshape(lines, 1, group)

    def second(g):
        part = pl.ds(g * group, group)
        wait_for(got_l.at[:, :, part], l_in.at[g])

        @pl.when(place == 1)
        def _():
            joint = lined(own_decay, g) * got_l[:, :, part].astype(F32) + l_send[:, :, part].astype(F32)
            i_send[:, :, part] = joint.astype(BF16)
            pass_on(g)

    def finish(g, before_decay):
        part = pl.ds(g * group, group)
        wait_for(got_i.at[:, :, part], i_in.at[g])
        earlier = jnp.where(place == 1, 0.0, got_i[:, :, part].astype(F32))
        entering = lined(before_decay, g) * earlier + got_l[:, :, part].astype(F32)

        @pl.when(place == 2)
        def _():
            joint = lined(own_decay, g) * entering + l_send[:, :, part].astype(F32)
            i_send[:, :, part] = joint.astype(BF16)
            pass_on(g)

        carried = dot(c_lines, entering.reshape(lines * STATE, group).astype(BF16))
        y = near[:, part] + expand(from_start, spread[:, g * group : (g + 1) * group]) * carried
        y_send[:, :, :, part] = y.reshape(WINDOW, lines, 8, group).astype(BF16)
        for d in fro:
            send_col(
                y_send.at[middle + d, :, :, part], got_y.at[rows_of(me_col), :, part], y_out.at[g], y_in.at[g],
                around(me_col + d),
            )
        got_y[rows_of(me_col), :, part] = y_send[middle, :, :, part]

    for g in range(min(2, GROUPS)):
        enter(g)

    wait_for(got_f.at[pl.ds(0, tall - 1)], f_in.at[0])
    wait_for(got_t.at[pl.ds(0, tall - 1)], f_in.at[1])
    ends = jnp.concatenate([got_t[k, pl.ds(me_row, 1), :] for k in range(tall)], axis=0)
    decay = expand(jnp.exp2(ends[:, :HEADS]), spread, 3)
    carry = jnp.zeros((STATE, INNER), F32)
    for k in range(tall):
        s_send[k] = carry.astype(BF16)
        if k < tall - 1:
            carry = decay[k : k + 1] * carry + got_f[k].astype(F32)
    for q in row_peers:
        send_row(s_send.at[q], got_s.at[me_row], s_out, s_in, q)
    got_s[me_row] = s_send[me_row]

    def column_local():
        bar_col = jnp.where(same, 0.0, -1e30)
        scores_col = scores_of(c_col, b_col)
        run_col_t = transposed(run_col)
        skip_wide = expand(skip_ref[...], spread, 3)
        for pair in range(HEADS // 2):
            part = slice(pair * 128, pair * 128 + 128)
            top0, low0 = weights_of(run_col, run_col_t, scores_col, bar_col, 2 * pair)
            top1, low1 = weights_of(run_col, run_col_t, scores_col, bar_col, 2 * pair + 1)
            u = u_col[:, part]
            kept = skip_wide[:, part] * x_all[:, part]
            acc[:half, part] = jnp.where(lane < HEAD, dot(top0, u[:half]), dot(top1, u[:half])) + kept[:half]
            acc[half:, part] = jnp.where(lane < HEAD, dot(low0, u), dot(low1, u)) + kept[half:]

    for g in range(2, GROUPS):
        enter(g)
        if g == 2:
            column_local()
    if GROUPS <= 2:
        column_local()

    wait_for(got_e, e_in)
    before_decay = expand(got_e[:lines, :HEADS], spread, 3)
    second(0)
    for g in range(GROUPS):
        if g + 1 < GROUPS:
            second(g + 1)
        finish(g, before_decay)

    loads[4].wait()
    gate = gate_ref[...].astype(F32).reshape(tokens, INNER)
    act[...] = 0.5 * gate * (1.0 + jnp.tanh(0.5 * gate))

    wait_for(got_s.at[pl.ds(0, tall - 1)], s_in)
    entering_col = dot(c_wide, got_s[...].astype(F32).reshape(8 * STATE, INNER).astype(BF16))
    acc[...] += expand(jnp.exp2(run_col), spread) * entering_col

    power = jnp.zeros((tokens, 128), F32)
    for g in range(GROUPS):
        part = pl.ds(g * group, group)
        wait_for(got_y.at[pl.ds(0, (WINDOW - 1) * lines), :, part], y_in.at[g])
        y_row = got_y[:, :, part].astype(F32).reshape(tokens, group)
        v = (y_row + acc[:, part]) * act[:, part]
        mixed[:, part] = v
        for i in range(group // 128):
            w = v[:, i * 128 : i * 128 + 128]
            power += w * w
    scale = lax.rsqrt(jnp.sum(power, axis=1, keepdims=True) * (1.0 / INNER) + 1e-05)
    for i in range(INNER // 128):
        here = pl.ds(i * 128, 128)
        out_ref[:, :, here] = (mixed[:, here] * scale * gain_ref[i : i + 1, :]).reshape(tile_rows, 8, 128).astype(BF16)

    wait_near(got_bc, m_out.at[0])
    wait_near(got_dt, m_out.at[1])
    wait_for(f_send.at[pl.ds(0, tall - 1)], f_out.at[0])
    wait_for(got_t.at[pl.ds(0, tall - 1)], f_out.at[1])
    wait_for(s_send.at[pl.ds(0, tall - 1)], s_out)
    wait_for(e_send, e_out)
    for g in range(GROUPS):
        part = pl.ds(g * group, group)
        wait_near(got_x.at[:, :, :, part], x_out.at[g])
        wait_near(y_send.at[:, :, :, part], y_out.at[g])
        wait_for(l_send.at[:, :, part], l_out.at[g])
        wait_for(i_send.at[:, :, part], i_out.at[g])


def body(lanes, tall, x_in, gate_in, proj_bc, dt_raw, step_index, step_table, rates, skip, norm_gain):
    _, tile_rows, tile_cols, _ = x_in.shape
    tokens = tile_rows * tile_cols
    lines = tile_rows // WINDOW
    steps = step_table.shape[0]
    vmem = pl.BlockSpec(memory_space=pltpu.VMEM)
    smem = pl.BlockSpec(memory_space=pltpu.SMEM)
    hbm = pl.BlockSpec(memory_space=pl.ANY)
    dma = pltpu.SemaphoreType.DMA
    out = pl.pallas_call(
        functools.partial(kernel, lanes, tall),
        out_shape=pltpu.VMEM((tile_rows, 8, INNER), BF16),
        in_specs=[smem, hbm, vmem, vmem, vmem, hbm, hbm, hbm, hbm],
        out_specs=vmem,
        scratch_shapes=[
            pltpu.VMEM((2 * HEADS, steps), F32),
            pltpu.VMEM((tile_rows, 8, INNER), BF16),
            pltpu.VMEM((tile_rows, 8, INNER), BF16),
            pltpu.VMEM((tile_rows, 8, 4 * STATE), BF16),
            pltpu.VMEM((tile_rows, 8, 2 * HEADS), BF16),
            dma((5,)),
            pltpu.VMEM((WINDOW, lines, 8, INNER), BF16),
            pltpu.VMEM((WINDOW, lines, 8, 4 * STATE), BF16),
            pltpu.VMEM((WINDOW, lines, 8, 2 * HEADS), BF16),
            pltpu.VMEM((WINDOW, lines, 8, INNER), BF16),
            pltpu.VMEM((tile_rows, 8, INNER), BF16),
            pltpu.VMEM((8, STATE, INNER), BF16),
            pltpu.VMEM((tall, STATE, INNER), BF16),
            pltpu.VMEM((8, 128), F32),
            pltpu.VMEM((tall, 8, 128), F32),
            pltpu.VMEM((tall, STATE, INNER), BF16),
            pltpu.VMEM((8, STATE, INNER), BF16),
            pltpu.VMEM((lines, STATE, INNER), BF16),
            pltpu.VMEM((lines, STATE, INNER), BF16),
            pltpu.VMEM((lines, STATE, INNER), BF16),
            pltpu.VMEM((lines, STATE, INNER), BF16),
            pltpu.VMEM((8, 128), F32),
            pltpu.VMEM((8, 128), F32),
            pltpu.VMEM((HEADS, tokens, tokens), BF16),
            pltpu.VMEM((tokens, INNER), F32),
            pltpu.VMEM((tokens, INNER), F32),
            pltpu.VMEM((tokens, INNER), F32),
            pltpu.VMEM((tokens, INNER), F32),
            pltpu.VMEM((tokens, INNER), F32),
            pltpu.VMEM((tokens, INNER), F32),
            dma((GROUPS,)),
            dma((GROUPS,)),
            dma((2,)),
            dma((2,)),
            dma((GROUPS,)),
            dma((GROUPS,)),
            dma((2,)),
            dma((2,)),
            dma,
            dma,
            dma((GROUPS,)),
            dma((GROUPS,)),
            dma((GROUPS,)),
            dma((GROUPS,)),
            dma,
            dma,
            pltpu.SemaphoreType.REGULAR,
        ],
        compiler_params=pltpu.CompilerParams(
            collective_id=0, has_side_effects=True, vmem_limit_bytes=60 * 1024 * 1024
        ),
    )(
        step_index,
        step_table.T,
        rates,
        skip.reshape(1, HEADS),
        norm_gain.reshape(INNER // 128, 128),
        x_in.reshape(tile_rows, 8, INNER),
        gate_in.reshape(tile_rows, 8, INNER),
        proj_bc.reshape(tile_rows, 8, 4 * STATE),
        dt_raw.reshape(tile_rows, 8, 2 * HEADS),
    )
    return out.reshape(x_in.shape)


def solution(mesh):
    tile = P("img", "row", "col", None)
    return jax.shard_map(
        functools.partial(body, mesh.shape["col"], mesh.shape["row"]),
        mesh=mesh,
        in_specs=(tile, tile, tile, tile, P("img"), P(), P(), P(), P()),
        out_specs=tile,
        check_vma=False,
    )
```

```python
import functools

import jax
import jax.numpy as jnp
from jax import lax
from jax.experimental import pallas as pl
from jax.experimental.pallas import tpu as pltpu
from jax.sharding import PartitionSpec as P

HEADS = 24
HEAD = 64
STATE = 16
INNER = HEADS * HEAD
GROUPS = 6
WINDOW = 8
LOG2E = 1.4426950408889634
F32 = jnp.float32
BF16 = jnp.bfloat16


def dot(a, b):
    return jnp.dot(a, b, preferred_element_type=F32)


def split(v, pieces):
    parts = []
    for _ in range(pieces):
        part = v.astype(BF16)
        parts.append(part)
        v = v - part.astype(F32)
    return parts


def dot_exact(zero_one, v, pieces=3):
    return sum(dot(zero_one, part) for part in split(v, pieces))


def expand(v, heads_to_channels, pieces=2):
    return sum(dot(part, heads_to_channels) for part in split(v, pieces))


def softplus(v):
    return jnp.maximum(v, 0.0) + jnp.log(1.0 + jnp.exp(-jnp.abs(v)))


def kernel(
    lanes, tall, step_ref, table_hbm, rates_ref, skip_ref, gain_ref, x_hbm, gate_hbm, bc_hbm, dt_hbm, out_ref,
    table_ref, x_ref, gate_ref, bc_ref, dt_ref, load_sem,
    got_x, got_bc, got_dt, y_send, got_y, f_send, got_f, t_send, got_t, s_send, got_s,
    l_send, got_l, i_send, got_i, e_send, got_e, w_row, u_row_s, end_s, near, acc, act, mixed,
    x_out, x_in, m_out, m_in, y_out, y_in, f_out, f_in, s_out, s_in, l_out, l_in, i_out, i_in, e_out, e_in, known,
):
    tile_rows = x_ref.shape[0]
    tokens = tile_rows * 8
    half = tokens // 2
    windows = lanes // WINDOW
    lines = tile_rows // WINDOW
    group = INNER // GROUPS
    group_heads = HEADS // GROUPS
    reach = WINDOW // 2
    flip = lax.axis_index("img") % 2
    middle = reach - flip
    sense = 1 - 2 * flip
    me_col = lax.axis_index("col")
    me_row = lax.axis_index("row")

    def around(c):
        return (c + 2 * lanes) % lanes

    def rows_of(c):
        return pl.ds(((c + WINDOW - middle) % WINDOW) * lines, lines)

    order = sorted(range(1, reach + 1), reverse=True)
    offsets = [d for k in order for d in ((k, -k) if k < reach else (k,))]
    to = [sense * d for d in offsets]
    fro = [-sense * d for d in offsets]
    row_peers = [(me_row + k) % tall for k in range(1, tall)]
    after, before, across = around(me_col + WINDOW), around(me_col - WINDOW), around(me_col + 2 * WINDOW)
    place = (around(me_col - middle + WINDOW - 1)) // WINDOW
    cut = around(middle - me_col)
    cut_in = jnp.where(place == 0, cut, WINDOW)
    cut_out = jnp.where(place == 0, cut, 0)

    barrier = pltpu.get_barrier_semaphore()

    def greet(**device):
        pl.semaphore_signal(barrier, inc=1, device_id=device, device_id_type=pl.DeviceIdType.MESH)

    greeted = [around(me_col + d) for k in order for d in (k, -k)] + ([across] if windows > 2 else [])
    for c in greeted:
        greet(col=c)
    for q in row_peers:
        greet(row=q)

    loads = []
    for i, (src, dst) in enumerate(
        ((bc_hbm, bc_ref), (dt_hbm, dt_ref), (table_hbm, table_ref), (x_hbm, x_ref), (gate_hbm, gate_ref))
    ):
        loads.append(pltpu.make_async_copy(src, dst, load_sem.at[i]))
        loads[-1].start()

    def send_col(src, dst, out_sem, in_sem, p):
        pltpu.make_async_remote_copy(
            src_ref=src, dst_ref=dst, send_sem=out_sem, recv_sem=in_sem,
            device_id={"col": p}, device_id_type=pl.DeviceIdType.MESH,
        ).start()

    def send_row(src, dst, out_sem, in_sem, q):
        pltpu.make_async_remote_copy(
            src_ref=src, dst_ref=dst, send_sem=out_sem, recv_sem=in_sem,
            device_id={"row": q}, device_id_type=pl.DeviceIdType.MESH,
        ).start()

    def wait_for(ref, sem):
        pltpu.make_async_copy(ref, ref, sem).wait()

    def send_states():
        for q in row_peers:
            send_row(f_send.at[q], got_f.at[me_row], f_out.at[0], f_in.at[0], q)
            send_row(t_send, got_t.at[me_row], f_out.at[1], f_in.at[1], q)

    def send_small(d):
        c = around(me_col + d)
        send_col(bc_ref.at[rows_of(c)], got_bc.at[middle - d], m_out.at[0], m_in.at[0], c)
        send_col(dt_ref.at[rows_of(c)], got_dt.at[middle - d], m_out.at[1], m_in.at[1], c)

    def send_tokens(g):
        part = pl.ds(g * group, group)
        for d in to:
            c = around(me_col + d)
            send_col(x_ref.at[rows_of(c), :, part], got_x.at[middle - d, :, :, part], x_out.at[g], x_in.at[g], c)

    pl.semaphore_wait(barrier, len(greeted) + tall - 1)

    for i in (0, 1, 3):
        loads[i].wait()
    for d in to:
        send_small(d)
    for g in range(GROUPS):
        send_tokens(g)
    pl.semaphore_signal(known, inc=1, device_id={"col": around(me_col - reach)}, device_id_type=pl.DeviceIdType.MESH)
    rows = lax.broadcasted_iota(jnp.int32, (tokens, tokens), 0)
    cols = lax.broadcasted_iota(jnp.int32, (tokens, tokens), 1)
    causal = rows >= cols
    same = causal & ((rows & 7) == (cols & 7))
    channel = lax.broadcasted_iota(jnp.int32, (HEADS, INNER), 1)
    head = lax.broadcasted_iota(jnp.int32, (HEADS, INNER), 0)
    spread = ((channel >= head * HEAD) & (channel < (head + 1) * HEAD)).astype(BF16)

    def widen(v, kept, count):
        wide = count * STATE
        fan = (
            (lax.broadcasted_iota(jnp.int32, (STATE, wide), 1) & (STATE - 1))
            == lax.broadcasted_iota(jnp.int32, (STATE, wide), 0)
        ).astype(BF16)
        return jnp.where(kept, dot(v, fan), 0.0)

    loads[2].wait()
    chosen = (lax.broadcasted_iota(jnp.int32, (8, table_ref.shape[1]), 1) == step_ref[0]).astype(BF16)
    bias = sum(
        lax.dot_general(chosen, part, (((1,), (1,)), ((), ())), preferred_element_type=F32)
        for part in split(table_ref[...], 3)
    )[0:1]
    dt_own = dt_ref[...].astype(F32).reshape(tokens, 2 * HEADS)
    dt_col = softplus(dt_own[:, HEADS:] + bias[:, HEADS:])
    log_col = dt_col * (-LOG2E * rates_ref[1:2, :])
    run_col = dot_exact(same.astype(BF16), log_col)
    run3 = run_col.reshape(tile_rows, 8, HEADS)
    end_col = run3[tile_rows - 1]
    to_end = jnp.exp2(end_col[None] - run3).reshape(tokens, HEADS)
    x_all = x_ref[...].astype(F32).reshape(tokens, INNER)
    u_col = (expand(dt_col, spread) * x_all).astype(BF16)
    bc_own = bc_ref[...].astype(F32).reshape(tokens, 4 * STATE)
    b_col = bc_own[:, 2 * STATE : 3 * STATE].astype(BF16)
    c_col = bc_own[:, 3 * STATE :].astype(BF16)
    own_col = (lax.broadcasted_iota(jnp.int32, (tokens, 8 * STATE), 1) // STATE) == (
        lax.broadcasted_iota(jnp.int32, (tokens, 8 * STATE), 0) & 7
    )
    c_wide = widen(c_col, own_col, 8).astype(BF16)
    u_end = (expand(to_end, spread) * u_col.astype(F32)).astype(BF16)
    states = dot(widen(b_col, own_col, 8).T.astype(BF16), u_end)
    f_send[...] = states.astype(BF16).reshape(8, STATE, INNER)
    t_send[...] = jnp.concatenate([end_col, jnp.zeros((8, 128 - HEADS), F32)], axis=1)

    send_states()
    got_f[me_row] = f_send[me_row]
    got_t[me_row] = t_send[...]
    got_bc[middle] = bc_ref[rows_of(me_col)]
    got_dt[middle] = dt_ref[rows_of(me_col)]
    got_x[middle] = x_ref[rows_of(me_col)]

    def wait_near(ref, sem):
        wait_for(ref.at[pl.ds(0, WINDOW - 1)], sem)

    def weights_of(run, run_t, scores, bar, h):
        top = jnp.exp2(run[:half, h : h + 1] - run_t[h : h + 1, :half] + bar[:half, :half]) * scores[:half, :half]
        low = jnp.exp2(run[half:, h : h + 1] - run_t[h : h + 1, :] + bar[half:, :]) * scores[half:, :]
        return top.astype(BF16), low.astype(BF16)

    def transposed(run):
        return jnp.concatenate([run, jnp.zeros((tokens, 128 - HEADS), F32)], axis=1).T

    def scores_of(c, b):
        return lax.dot_general(c, b, (((1,), (1,)), ((), ())), preferred_element_type=F32)

    lane = lax.broadcasted_iota(jnp.int32, (1, 128), 1)

    wait_near(got_bc, m_in.at[0])
    wait_near(got_dt, m_in.at[1])
    pl.semaphore_wait(known, 1)
    line_size = 8 * lines
    tile_i, tile_j = rows // line_size, cols // line_size
    line_i, line_j = (rows // 8) % lines, (cols // 8) % lines
    joined = causal & (line_i == line_j) & ((tile_i >= cut_out) == (tile_j >= cut_out))
    bc_line = got_bc[...].astype(F32).reshape(tokens, 4 * STATE)
    dt_line = got_dt[...].astype(F32).reshape(tokens, 2 * HEADS)
    dt_row = softplus(dt_line[:, :HEADS] + bias[:, :HEADS])
    log_row = dt_row * (-LOG2E * rates_ref[0:1, :])
    run_row = dot_exact(joined.astype(BF16), log_row)
    ends_row = run_row.reshape(WINDOW, lines, 8, HEADS)[WINDOW - 1, :, 7:8, :]
    run4 = run_row.reshape(WINDOW, lines, 8, HEADS)
    tile4 = lax.broadcasted_iota(jnp.int32, (WINDOW, lines, 8, HEADS), 0)
    to_end_row = jnp.where(tile4 >= cut_out, jnp.exp2(ends_row[None] - run4), 0.0).reshape(tokens, HEADS)
    from_start = jnp.where(tile4 < cut_in, jnp.exp2(run4), 0.0).reshape(tokens, HEADS)
    own_line = (lax.broadcasted_iota(jnp.int32, (tokens, lines * STATE), 1) // STATE) == (
        lax.broadcasted_iota(jnp.int32, (tokens, lines * STATE), 0) // 8
    ) % lines
    b_row = bc_line[:, :STATE].astype(BF16)
    c_row = bc_line[:, STATE : 2 * STATE].astype(BF16)
    b_lines = widen(b_row, own_line, lines).T.astype(BF16)
    c_lines = widen(c_row, own_line, lines).astype(BF16)
    u_row_s[...] = expand(dt_row, spread)
    end_s[...] = expand(to_end_row, spread)
    line_decay = jnp.exp2(ends_row.reshape(lines, HEADS))
    e_send[...] = jnp.concatenate(
        [
            jnp.concatenate([line_decay, jnp.zeros((8 - lines, HEADS), F32)], axis=0),
            jnp.zeros((8, 128 - HEADS), F32),
        ],
        axis=1,
    )
    own_decay = expand(line_decay, spread, 3)
    send_col(e_send, got_e, e_out, e_in, after)
    scores_row = scores_of(c_row, b_row)
    run_row_t = transposed(run_row)
    bar_row = jnp.where(joined, 0.0, -1e30)
    for h in range(HEADS):
        top, low = weights_of(run_row, run_row_t, scores_row, bar_row, h)
        w_row[h, :half, :half] = top
        w_row[h, half:, :] = low

    def enter(g):
        part = pl.ds(g * group, group)
        wait_near(got_x.at[:, :, :, part], x_in.at[g])
        x_line = got_x[:, :, :, part].astype(F32).reshape(tokens, group)
        u = (u_row_s[:, part] * x_line).astype(BF16)
        u_end = (end_s[:, part] * u.astype(F32)).astype(BF16)
        state = dot(b_lines, u_end)
        l_send[:, :, part] = state.reshape(lines, STATE, group).astype(BF16)
        send_col(l_send.at[:, :, part], got_l.at[:, :, part], l_out.at[g], l_in.at[g], after)

        @pl.when((place == 0) | (place == windows - 1))
        def _():
            i_send[:, :, part] = state.reshape(lines, STATE, group).astype(BF16)
            pass_on(g)

        for i in range(group_heads // 2):
            h = g * group_heads + 2 * i
            u_pair = u[:, i * 128 : i * 128 + 128]
            here = pl.ds(h * HEAD, 128)
            near[:half, here] = jnp.where(
                lane < HEAD, dot(w_row[h, :half, :half], u_pair[:half]), dot(w_row[h + 1, :half, :half], u_pair[:half])
            )
            near[half:, here] = jnp.where(
                lane < HEAD, dot(w_row[h, half:, :], u_pair), dot(w_row[h + 1, half:, :], u_pair)
            )

    def pass_on(g):
        part = pl.ds(g * group, group)
        send_col(i_send.at[:, :, part], got_i.at[:, :, part], i_out.at[g], i_in.at[g], across)

    def lined(v, g):
        return v[:, g * group : (g + 1) * group].reshape(lines, 1, group)

    def second(g):
        part = pl.ds(g * group, group)
        wait_for(got_l.at[:, :, part], l_in.at[g])

        @pl.when(place == 1)
        def _():
            joint = lined(own_decay, g) * got_l[:, :, part].astype(F32) + l_send[:, :, part].astype(F32)
            i_send[:, :, part] = joint.astype(BF16)
            pass_on(g)

    def finish(g, before_decay):
        part = pl.ds(g * group, group)
        wait_for(got_i.at[:, :, part], i_in.at[g])
        earlier = jnp.where(place == 1, 0.0, got_i[:, :, part].astype(F32))
        entering = lined(before_decay, g) * earlier + got_l[:, :, part].astype(F32)

        @pl.when(place == 2)
        def _():
            joint = lined(own_decay, g) * entering + l_send[:, :, part].astype(F32)
            i_send[:, :, part] = joint.astype(BF16)
            pass_on(g)

        carried = dot(c_lines, entering.reshape(lines * STATE, group).astype(BF16))
        y = near[:, part] + expand(from_start, spread[:, g * group : (g + 1) * group]) * carried
        y_send[:, :, :, part] = y.reshape(WINDOW, lines, 8, group).astype(BF16)
        for d in fro:
            send_col(
                y_send.at[middle + d, :, :, part], got_y.at[rows_of(me_col), :, part], y_out.at[g], y_in.at[g],
                around(me_col + d),
            )
        got_y[rows_of(me_col), :, part] = y_send[middle, :, :, part]

    for g in range(min(2, GROUPS)):
        enter(g)

    wait_for(got_f.at[pl.ds(0, tall - 1)], f_in.at[0])
    wait_for(got_t.at[pl.ds(0, tall - 1)], f_in.at[1])
    ends = jnp.concatenate([got_t[k, pl.ds(me_row, 1), :] for k in range(tall)], axis=0)
    decay = expand(jnp.exp2(ends[:, :HEADS]), spread, 3)
    carry = jnp.zeros((STATE, INNER), F32)
    for k in range(tall):
        s_send[k] = carry.astype(BF16)
        if k < tall - 1:
            carry = decay[k : k + 1] * carry + got_f[k].astype(F32)
    for q in row_peers:
        send_row(s_send.at[q], got_s.at[me_row], s_out, s_in, q)
    got_s[me_row] = s_send[me_row]

    def column_local():
        bar_col = jnp.where(same, 0.0, -1e30)
        scores_col = scores_of(c_col, b_col)
        run_col_t = transposed(run_col)
        skip_wide = expand(skip_ref[...], spread, 3)
        for pair in range(HEADS // 2):
            part = slice(pair * 128, pair * 128 + 128)
            top0, low0 = weights_of(run_col, run_col_t, scores_col, bar_col, 2 * pair)
            top1, low1 = weights_of(run_col, run_col_t, scores_col, bar_col, 2 * pair + 1)
            u = u_col[:, part]
            kept = skip_wide[:, part] * x_all[:, part]
            acc[:half, part] = jnp.where(lane < HEAD, dot(top0, u[:half]), dot(top1, u[:half])) + kept[:half]
            acc[half:, part] = jnp.where(lane < HEAD, dot(low0, u), dot(low1, u)) + kept[half:]

    for g in range(2, GROUPS):
        enter(g)
        if g == 2:
            column_local()
    if GROUPS <= 2:
        column_local()

    wait_for(got_e, e_in)
    before_decay = expand(got_e[:lines, :HEADS], spread, 3)
    second(0)
    for g in range(GROUPS):
        if g + 1 < GROUPS:
            second(g + 1)
        finish(g, before_decay)

    loads[4].wait()
    gate = gate_ref[...].astype(F32).reshape(tokens, INNER)
    act[...] = 0.5 * gate * (1.0 + jnp.tanh(0.5 * gate))

    wait_for(got_s.at[pl.ds(0, tall - 1)], s_in)
    entering_col = dot(c_wide, got_s[...].astype(F32).reshape(8 * STATE, INNER).astype(BF16))
    acc[...] += expand(jnp.exp2(run_col), spread) * entering_col

    power = jnp.zeros((tokens, 128), F32)
    for g in range(GROUPS):
        part = pl.ds(g * group, group)
        wait_for(got_y.at[pl.ds(0, (WINDOW - 1) * lines), :, part], y_in.at[g])
        y_row = got_y[:, :, part].astype(F32).reshape(tokens, group)
        v = (y_row + acc[:, part]) * act[:, part]
        mixed[:, part] = v
        for i in range(group // 128):
            w = v[:, i * 128 : i * 128 + 128]
            power += w * w
    scale = lax.rsqrt(jnp.sum(power, axis=1, keepdims=True) * (1.0 / INNER) + 1e-05)
    for i in range(INNER // 128):
        here = pl.ds(i * 128, 128)
        out_ref[:, :, here] = (mixed[:, here] * scale * gain_ref[i : i + 1, :]).reshape(tile_rows, 8, 128).astype(BF16)

    wait_near(got_bc, m_out.at[0])
    wait_near(got_dt, m_out.at[1])
    wait_for(f_send.at[pl.ds(0, tall - 1)], f_out.at[0])
    wait_for(got_t.at[pl.ds(0, tall - 1)], f_out.at[1])
    wait_for(s_send.at[pl.ds(0, tall - 1)], s_out)
    wait_for(e_send, e_out)
    for g in range(GROUPS):
        part = pl.ds(g * group, group)
        wait_near(got_x.at[:, :, :, part], x_out.at[g])
        wait_near(y_send.at[:, :, :, part], y_out.at[g])
        wait_for(l_send.at[:, :, part], l_out.at[g])
        wait_for(i_send.at[:, :, part], i_out.at[g])


def body(lanes, tall, x_in, gate_in, proj_bc, dt_raw, step_index, step_table, rates, skip, norm_gain):
    _, tile_rows, tile_cols, _ = x_in.shape
    tokens = tile_rows * tile_cols
    lines = tile_rows // WINDOW
    steps = step_table.shape[0]
    vmem = pl.BlockSpec(memory_space=pltpu.VMEM)
    smem = pl.BlockSpec(memory_space=pltpu.SMEM)
    hbm = pl.BlockSpec(memory_space=pl.ANY)
    dma = pltpu.SemaphoreType.DMA
    out = pl.pallas_call(
        functools.partial(kernel, lanes, tall),
        out_shape=pltpu.VMEM((tile_rows, 8, INNER), BF16),
        in_specs=[smem, hbm, vmem, vmem, vmem, hbm, hbm, hbm, hbm],
        out_specs=vmem,
        scratch_shapes=[
            pltpu.VMEM((2 * HEADS, steps), F32),
            pltpu.VMEM((tile_rows, 8, INNER), BF16),
            pltpu.VMEM((tile_rows, 8, INNER), BF16),
            pltpu.VMEM((tile_rows, 8, 4 * STATE), BF16),
            pltpu.VMEM((tile_rows, 8, 2 * HEADS), BF16),
            dma((5,)),
            pltpu.VMEM((WINDOW, lines, 8, INNER), BF16),
            pltpu.VMEM((WINDOW, lines, 8, 4 * STATE), BF16),
            pltpu.VMEM((WINDOW, lines, 8, 2 * HEADS), BF16),
            pltpu.VMEM((WINDOW, lines, 8, INNER), BF16),
            pltpu.VMEM((tile_rows, 8, INNER), BF16),
            pltpu.VMEM((8, STATE, INNER), BF16),
            pltpu.VMEM((tall, STATE, INNER), BF16),
            pltpu.VMEM((8, 128), F32),
            pltpu.VMEM((tall, 8, 128), F32),
            pltpu.VMEM((tall, STATE, INNER), BF16),
            pltpu.VMEM((8, STATE, INNER), BF16),
            pltpu.VMEM((lines, STATE, INNER), BF16),
            pltpu.VMEM((lines, STATE, INNER), BF16),
            pltpu.VMEM((lines, STATE, INNER), BF16),
            pltpu.VMEM((lines, STATE, INNER), BF16),
            pltpu.VMEM((8, 128), F32),
            pltpu.VMEM((8, 128), F32),
            pltpu.VMEM((HEADS, tokens, tokens), BF16),
            pltpu.VMEM((tokens, INNER), F32),
            pltpu.VMEM((tokens, INNER), F32),
            pltpu.VMEM((tokens, INNER), F32),
            pltpu.VMEM((tokens, INNER), F32),
            pltpu.VMEM((tokens, INNER), F32),
            pltpu.VMEM((tokens, INNER), F32),
            dma((GROUPS,)),
            dma((GROUPS,)),
            dma((2,)),
            dma((2,)),
            dma((GROUPS,)),
            dma((GROUPS,)),
            dma((2,)),
            dma((2,)),
            dma,
            dma,
            dma((GROUPS,)),
            dma((GROUPS,)),
            dma((GROUPS,)),
            dma((GROUPS,)),
            dma,
            dma,
            pltpu.SemaphoreType.REGULAR,
        ],
        compiler_params=pltpu.CompilerParams(
            collective_id=0, has_side_effects=True, vmem_limit_bytes=60 * 1024 * 1024
        ),
    )(
        step_index,
        step_table.T,
        rates,
        skip.reshape(1, HEADS),
        norm_gain.reshape(INNER // 128, 128),
        x_in.reshape(tile_rows, 8, INNER),
        gate_in.reshape(tile_rows, 8, INNER),
        proj_bc.reshape(tile_rows, 8, 4 * STATE),
        dt_raw.reshape(tile_rows, 8, 2 * HEADS),
    )
    return out.reshape(x_in.shape)


def solution(mesh):
    tile = P("img", "row", "col", None)
    return jax.shard_map(
        functools.partial(body, mesh.shape["col"], mesh.shape["row"]),
        mesh=mesh,
        in_specs=(tile, tile, tile, tile, P("img"), P(), P(), P(), P()),
        out_specs=tile,
        check_vma=False,
    )
```

```python
import functools

import jax
import jax.numpy as jnp
from jax import lax
from jax.experimental import pallas as pl
from jax.experimental.pallas import tpu as pltpu
from jax.sharding import PartitionSpec as P

HEADS = 24
HEAD = 64
STATE = 16
INNER = HEADS * HEAD
GROUPS = 6
WINDOW = 8
LAG = 3
LOG2E = 1.4426950408889634
F32 = jnp.float32
BF16 = jnp.bfloat16


def dot(a, b):
    return jnp.dot(a, b, preferred_element_type=F32)


def split(v, pieces):
    parts = []
    for _ in range(pieces):
        part = v.astype(BF16)
        parts.append(part)
        v = v - part.astype(F32)
    return parts


def dot_exact(zero_one, v, pieces=3):
    return sum(dot(zero_one, part) for part in split(v, pieces))


def expand(v, heads_to_channels, pieces=2):
    return sum(dot(part, heads_to_channels) for part in split(v, pieces))


def softplus(v):
    return jnp.maximum(v, 0.0) + jnp.log(1.0 + jnp.exp(-jnp.abs(v)))


def kernel(
    lanes, tall, step_ref, table_hbm, rates_ref, skip_ref, gain_ref, x_hbm, gate_hbm, bc_hbm, dt_hbm, out_ref,
    table_ref, x_ref, gate_ref, bc_ref, dt_ref, load_sem,
    got_x, got_bc, got_dt, y_send, got_y, f_send, got_f, t_send, got_t, s_send, got_s,
    l_send, got_l, i_send, got_i, e_send, got_e, w_row, u_row_s, end_s, near, acc, act, mixed,
    x_out, x_in, m_out, m_in, y_out, y_in, f_out, f_in, s_out, s_in, l_out, l_in, i_out, i_in, e_out, e_in, known,
):
    tile_rows = x_ref.shape[0]
    tokens = tile_rows * 8
    half = tokens // 2
    windows = lanes // WINDOW
    lines = tile_rows // WINDOW
    group = INNER // GROUPS
    group_heads = HEADS // GROUPS
    reach = WINDOW // 2
    flip = lax.axis_index("img") % 2
    middle = reach - flip
    sense = 1 - 2 * flip
    me_col = lax.axis_index("col")
    me_row = lax.axis_index("row")

    def around(c):
        return (c + 2 * lanes) % lanes

    def rows_of(c):
        return pl.ds(((c + WINDOW - middle) % WINDOW) * lines, lines)

    order = sorted(range(1, reach + 1), reverse=True)
    offsets = [d for k in order for d in ((k, -k) if k < reach else (k,))]
    to = [sense * d for d in offsets]
    fro = [-sense * d for d in offsets]
    row_peers = [(me_row + k) % tall for k in range(1, tall)]
    after, before, across = around(me_col + WINDOW), around(me_col - WINDOW), around(me_col + 2 * WINDOW)
    place = (around(me_col - middle + WINDOW - 1)) // WINDOW
    cut = around(middle - me_col)
    cut_in = jnp.where(place == 0, cut, WINDOW)
    cut_out = jnp.where(place == 0, cut, 0)

    barrier = pltpu.get_barrier_semaphore()

    def greet(**device):
        pl.semaphore_signal(barrier, inc=1, device_id=device, device_id_type=pl.DeviceIdType.MESH)

    greeted = [around(me_col + d) for k in order for d in (k, -k)] + ([across] if windows > 2 else [])
    for c in greeted:
        greet(col=c)
    for q in row_peers:
        greet(row=q)

    loads = []
    for i, (src, dst) in enumerate(
        ((bc_hbm, bc_ref), (dt_hbm, dt_ref), (table_hbm, table_ref), (x_hbm, x_ref), (gate_hbm, gate_ref))
    ):
        loads.append(pltpu.make_async_copy(src, dst, load_sem.at[i]))
        loads[-1].start()

    def send_col(src, dst, out_sem, in_sem, p):
        pltpu.make_async_remote_copy(
            src_ref=src, dst_ref=dst, send_sem=out_sem, recv_sem=in_sem,
            device_id={"col": p}, device_id_type=pl.DeviceIdType.MESH,
        ).start()

    def send_row(src, dst, out_sem, in_sem, q):
        pltpu.make_async_remote_copy(
            src_ref=src, dst_ref=dst, send_sem=out_sem, recv_sem=in_sem,
            device_id={"row": q}, device_id_type=pl.DeviceIdType.MESH,
        ).start()

    def wait_for(ref, sem):
        pltpu.make_async_copy(ref, ref, sem).wait()

    def send_states():
        for q in row_peers:
            send_row(f_send.at[q], got_f.at[me_row], f_out.at[0], f_in.at[0], q)
            send_row(t_send, got_t.at[me_row], f_out.at[1], f_in.at[1], q)

    def send_small(d):
        c = around(me_col + d)
        send_col(bc_ref.at[rows_of(c)], got_bc.at[middle - d], m_out.at[0], m_in.at[0], c)
        send_col(dt_ref.at[rows_of(c)], got_dt.at[middle - d], m_out.at[1], m_in.at[1], c)

    def send_tokens(g):
        part = pl.ds(g * group, group)
        for d in to:
            c = around(me_col + d)
            send_col(x_ref.at[rows_of(c), :, part], got_x.at[middle - d, :, :, part], x_out.at[g], x_in.at[g], c)

    pl.semaphore_wait(barrier, len(greeted) + tall - 1)

    for i in (0, 1, 3):
        loads[i].wait()
    for d in to:
        send_small(d)
    for g in range(GROUPS):
        send_tokens(g)
    pl.semaphore_signal(known, inc=1, device_id={"col": around(me_col - reach)}, device_id_type=pl.DeviceIdType.MESH)
    rows = lax.broadcasted_iota(jnp.int32, (tokens, tokens), 0)
    cols = lax.broadcasted_iota(jnp.int32, (tokens, tokens), 1)
    causal = rows >= cols
    same = causal & ((rows & 7) == (cols & 7))
    channel = lax.broadcasted_iota(jnp.int32, (HEADS, INNER), 1)
    head = lax.broadcasted_iota(jnp.int32, (HEADS, INNER), 0)
    spread = ((channel >= head * HEAD) & (channel < (head + 1) * HEAD)).astype(BF16)

    def widen(v, kept, count):
        wide = count * STATE
        fan = (
            (lax.broadcasted_iota(jnp.int32, (STATE, wide), 1) & (STATE - 1))
            == lax.broadcasted_iota(jnp.int32, (STATE, wide), 0)
        ).astype(BF16)
        return jnp.where(kept, dot(v, fan), 0.0)

    loads[2].wait()
    chosen = (lax.broadcasted_iota(jnp.int32, (8, table_ref.shape[1]), 1) == step_ref[0]).astype(BF16)
    bias = sum(
        lax.dot_general(chosen, part, (((1,), (1,)), ((), ())), preferred_element_type=F32)
        for part in split(table_ref[...], 3)
    )[0:1]
    dt_own = dt_ref[...].astype(F32).reshape(tokens, 2 * HEADS)
    dt_col = softplus(dt_own[:, HEADS:] + bias[:, HEADS:])
    log_col = dt_col * (-LOG2E * rates_ref[1:2, :])
    run_col = dot_exact(same.astype(BF16), log_col)
    run3 = run_col.reshape(tile_rows, 8, HEADS)
    end_col = run3[tile_rows - 1]
    to_end = jnp.exp2(end_col[None] - run3).reshape(tokens, HEADS)
    x_all = x_ref[...].astype(F32).reshape(tokens, INNER)
    u_col = (expand(dt_col, spread) * x_all).astype(BF16)
    bc_own = bc_ref[...].astype(F32).reshape(tokens, 4 * STATE)
    b_col = bc_own[:, 2 * STATE : 3 * STATE].astype(BF16)
    c_col = bc_own[:, 3 * STATE :].astype(BF16)
    own_col = (lax.broadcasted_iota(jnp.int32, (tokens, 8 * STATE), 1) // STATE) == (
        lax.broadcasted_iota(jnp.int32, (tokens, 8 * STATE), 0) & 7
    )
    c_wide = widen(c_col, own_col, 8).astype(BF16)
    u_end = (expand(to_end, spread) * u_col.astype(F32)).astype(BF16)
    states = dot(widen(b_col, own_col, 8).T.astype(BF16), u_end)
    f_send[...] = states.astype(BF16).reshape(8, STATE, INNER)
    t_send[...] = jnp.concatenate([end_col, jnp.zeros((8, 128 - HEADS), F32)], axis=1)

    send_states()
    got_f[me_row] = f_send[me_row]
    got_t[me_row] = t_send[...]
    got_bc[middle] = bc_ref[rows_of(me_col)]
    got_dt[middle] = dt_ref[rows_of(me_col)]
    got_x[middle] = x_ref[rows_of(me_col)]

    def wait_near(ref, sem):
        wait_for(ref.at[pl.ds(0, WINDOW - 1)], sem)

    def weights_of(run, run_t, scores, bar, h):
        top = jnp.exp2(run[:half, h : h + 1] - run_t[h : h + 1, :half] + bar[:half, :half]) * scores[:half, :half]
        low = jnp.exp2(run[half:, h : h + 1] - run_t[h : h + 1, :] + bar[half:, :]) * scores[half:, :]
        return top.astype(BF16), low.astype(BF16)

    def transposed(run):
        return jnp.concatenate([run, jnp.zeros((tokens, 128 - HEADS), F32)], axis=1).T

    def scores_of(c, b):
        return lax.dot_general(c, b, (((1,), (1,)), ((), ())), preferred_element_type=F32)

    lane = lax.broadcasted_iota(jnp.int32, (1, 128), 1)

    wait_near(got_bc, m_in.at[0])
    wait_near(got_dt, m_in.at[1])
    pl.semaphore_wait(known, 1)
    line_size = 8 * lines
    tile_i, tile_j = rows // line_size, cols // line_size
    line_i, line_j = (rows // 8) % lines, (cols // 8) % lines
    joined = causal & (line_i == line_j) & ((tile_i >= cut_out) == (tile_j >= cut_out))
    bc_line = got_bc[...].astype(F32).reshape(tokens, 4 * STATE)
    dt_line = got_dt[...].astype(F32).reshape(tokens, 2 * HEADS)
    dt_row = softplus(dt_line[:, :HEADS] + bias[:, :HEADS])
    log_row = dt_row * (-LOG2E * rates_ref[0:1, :])
    run_row = dot_exact(joined.astype(BF16), log_row)
    ends_row = run_row.reshape(WINDOW, lines, 8, HEADS)[WINDOW - 1, :, 7:8, :]
    run4 = run_row.reshape(WINDOW, lines, 8, HEADS)
    tile4 = lax.broadcasted_iota(jnp.int32, (WINDOW, lines, 8, HEADS), 0)
    to_end_row = jnp.where(tile4 >= cut_out, jnp.exp2(ends_row[None] - run4), 0.0).reshape(tokens, HEADS)
    from_start = jnp.where(tile4 < cut_in, jnp.exp2(run4), 0.0).reshape(tokens, HEADS)
    own_line = (lax.broadcasted_iota(jnp.int32, (tokens, lines * STATE), 1) // STATE) == (
        lax.broadcasted_iota(jnp.int32, (tokens, lines * STATE), 0) // 8
    ) % lines
    b_row = bc_line[:, :STATE].astype(BF16)
    c_row = bc_line[:, STATE : 2 * STATE].astype(BF16)
    b_lines = widen(b_row, own_line, lines).T.astype(BF16)
    c_lines = widen(c_row, own_line, lines).astype(BF16)
    u_row_s[...] = expand(dt_row, spread)
    end_s[...] = expand(to_end_row, spread)
    line_decay = jnp.exp2(ends_row.reshape(lines, HEADS))
    e_send[...] = jnp.concatenate(
        [
            jnp.concatenate([line_decay, jnp.zeros((8 - lines, HEADS), F32)], axis=0),
            jnp.zeros((8, 128 - HEADS), F32),
        ],
        axis=1,
    )
    own_decay = expand(line_decay, spread, 3)
    send_col(e_send, got_e, e_out, e_in, after)
    scores_row = scores_of(c_row, b_row)
    run_row_t = transposed(run_row)
    bar_row = jnp.where(joined, 0.0, -1e30)
    for h in range(HEADS):
        top, low = weights_of(run_row, run_row_t, scores_row, bar_row, h)
        w_row[h, :half, :half] = top
        w_row[h, half:, :] = low

    def enter(g):
        part = pl.ds(g * group, group)
        wait_near(got_x.at[:, :, :, part], x_in.at[g])
        x_line = got_x[:, :, :, part].astype(F32).reshape(tokens, group)
        u = (u_row_s[:, part] * x_line).astype(BF16)
        u_end = (end_s[:, part] * u.astype(F32)).astype(BF16)
        state = dot(b_lines, u_end)
        l_send[:, :, part] = state.reshape(lines, STATE, group).astype(BF16)
        send_col(l_send.at[:, :, part], got_l.at[:, :, part], l_out.at[g], l_in.at[g], after)

        @pl.when((place == 0) | (place == windows - 1))
        def _():
            i_send[:, :, part] = state.reshape(lines, STATE, group).astype(BF16)
            pass_on(g)

        for i in range(group_heads // 2):
            h = g * group_heads + 2 * i
            u_pair = u[:, i * 128 : i * 128 + 128]
            here = pl.ds(h * HEAD, 128)
            near[:half, here] = jnp.where(
                lane < HEAD, dot(w_row[h, :half, :half], u_pair[:half]), dot(w_row[h + 1, :half, :half], u_pair[:half])
            )
            near[half:, here] = jnp.where(
                lane < HEAD, dot(w_row[h, half:, :], u_pair), dot(w_row[h + 1, half:, :], u_pair)
            )

    def pass_on(g):
        part = pl.ds(g * group, group)
        send_col(i_send.at[:, :, part], got_i.at[:, :, part], i_out.at[g], i_in.at[g], across)

    def lined(v, g):
        return v[:, g * group : (g + 1) * group].reshape(lines, 1, group)

    def second(g):
        part = pl.ds(g * group, group)
        wait_for(got_l.at[:, :, part], l_in.at[g])

        @pl.when(place == 1)
        def _():
            joint = lined(own_decay, g) * got_l[:, :, part].astype(F32) + l_send[:, :, part].astype(F32)
            i_send[:, :, part] = joint.astype(BF16)
            pass_on(g)

    def finish(g, before_decay):
        part = pl.ds(g * group, group)
        wait_for(got_i.at[:, :, part], i_in.at[g])
        earlier = jnp.where(place == 1, 0.0, got_i[:, :, part].astype(F32))
        entering = lined(before_decay, g) * earlier + got_l[:, :, part].astype(F32)

        @pl.when(place == 2)
        def _():
            joint = lined(own_decay, g) * entering + l_send[:, :, part].astype(F32)
            i_send[:, :, part] = joint.astype(BF16)
            pass_on(g)

        carried = dot(c_lines, entering.reshape(lines * STATE, group).astype(BF16))
        y = near[:, part] + expand(from_start, spread[:, g * group : (g + 1) * group]) * carried
        y_send[:, :, :, part] = y.reshape(WINDOW, lines, 8, group).astype(BF16)
        for d in fro:
            send_col(
                y_send.at[middle + d, :, :, part], got_y.at[rows_of(me_col), :, part], y_out.at[g], y_in.at[g],
                around(me_col + d),
            )
        got_y[rows_of(me_col), :, part] = y_send[middle, :, :, part]

    for g in range(min(2, GROUPS)):
        enter(g)

    wait_for(got_f.at[pl.ds(0, tall - 1)], f_in.at[0])
    wait_for(got_t.at[pl.ds(0, tall - 1)], f_in.at[1])
    ends = jnp.concatenate([got_t[k, pl.ds(me_row, 1), :] for k in range(tall)], axis=0)
    decay = expand(jnp.exp2(ends[:, :HEADS]), spread, 3)
    carry = jnp.zeros((STATE, INNER), F32)
    for k in range(tall):
        s_send[k] = carry.astype(BF16)
        if k < tall - 1:
            carry = decay[k : k + 1] * carry + got_f[k].astype(F32)
    for q in row_peers:
        send_row(s_send.at[q], got_s.at[me_row], s_out, s_in, q)
    got_s[me_row] = s_send[me_row]

    def column_local():
        bar_col = jnp.where(same, 0.0, -1e30)
        scores_col = scores_of(c_col, b_col)
        run_col_t = transposed(run_col)
        skip_wide = expand(skip_ref[...], spread, 3)
        for pair in range(HEADS // 2):
            part = slice(pair * 128, pair * 128 + 128)
            top0, low0 = weights_of(run_col, run_col_t, scores_col, bar_col, 2 * pair)
            top1, low1 = weights_of(run_col, run_col_t, scores_col, bar_col, 2 * pair + 1)
            u = u_col[:, part]
            kept = skip_wide[:, part] * x_all[:, part]
            acc[:half, part] = jnp.where(lane < HEAD, dot(top0, u[:half]), dot(top1, u[:half])) + kept[:half]
            acc[half:, part] = jnp.where(lane < HEAD, dot(low0, u), dot(low1, u)) + kept[half:]

    wait_for(got_e, e_in)
    before_decay = expand(got_e[:lines, :HEADS], spread, 3)

    for turn in range(2, GROUPS + LAG + 1):
        if turn < GROUPS:
            enter(turn)
        if turn == 2:
            column_local()
        if 0 <= turn - LAG < GROUPS:
            second(turn - LAG)
        if 0 <= turn - LAG - 1 < GROUPS:
            finish(turn - LAG - 1, before_decay)

    loads[4].wait()
    gate = gate_ref[...].astype(F32).reshape(tokens, INNER)
    act[...] = 0.5 * gate * (1.0 + jnp.tanh(0.5 * gate))

    wait_for(got_s.at[pl.ds(0, tall - 1)], s_in)
    entering_col = dot(c_wide, got_s[...].astype(F32).reshape(8 * STATE, INNER).astype(BF16))
    acc[...] += expand(jnp.exp2(run_col), spread) * entering_col

    power = jnp.zeros((tokens, 128), F32)
    for g in range(GROUPS):
        part = pl.ds(g * group, group)
        wait_for(got_y.at[pl.ds(0, (WINDOW - 1) * lines), :, part], y_in.at[g])
        y_row = got_y[:, :, part].astype(F32).reshape(tokens, group)
        v = (y_row + acc[:, part]) * act[:, part]
        mixed[:, part] = v
        for i in range(group // 128):
            w = v[:, i * 128 : i * 128 + 128]
            power += w * w
    scale = lax.rsqrt(jnp.sum(power, axis=1, keepdims=True) * (1.0 / INNER) + 1e-05)
    for i in range(INNER // 128):
        here = pl.ds(i * 128, 128)
        out_ref[:, :, here] = (mixed[:, here] * scale * gain_ref[i : i + 1, :]).reshape(tile_rows, 8, 128).astype(BF16)

    wait_near(got_bc, m_out.at[0])
    wait_near(got_dt, m_out.at[1])
    wait_for(f_send.at[pl.ds(0, tall - 1)], f_out.at[0])
    wait_for(got_t.at[pl.ds(0, tall - 1)], f_out.at[1])
    wait_for(s_send.at[pl.ds(0, tall - 1)], s_out)
    wait_for(e_send, e_out)
    for g in range(GROUPS):
        part = pl.ds(g * group, group)
        wait_near(got_x.at[:, :, :, part], x_out.at[g])
        wait_near(y_send.at[:, :, :, part], y_out.at[g])
        wait_for(l_send.at[:, :, part], l_out.at[g])
        wait_for(i_send.at[:, :, part], i_out.at[g])


def body(lanes, tall, x_in, gate_in, proj_bc, dt_raw, step_index, step_table, rates, skip, norm_gain):
    _, tile_rows, tile_cols, _ = x_in.shape
    tokens = tile_rows * tile_cols
    lines = tile_rows // WINDOW
    steps = step_table.shape[0]
    vmem = pl.BlockSpec(memory_space=pltpu.VMEM)
    smem = pl.BlockSpec(memory_space=pltpu.SMEM)
    hbm = pl.BlockSpec(memory_space=pl.ANY)
    dma = pltpu.SemaphoreType.DMA
    out = pl.pallas_call(
        functools.partial(kernel, lanes, tall),
        out_shape=pltpu.VMEM((tile_rows, 8, INNER), BF16),
        in_specs=[smem, hbm, vmem, vmem, vmem, hbm, hbm, hbm, hbm],
        out_specs=vmem,
        scratch_shapes=[
            pltpu.VMEM((2 * HEADS, steps), F32),
            pltpu.VMEM((tile_rows, 8, INNER), BF16),
            pltpu.VMEM((tile_rows, 8, INNER), BF16),
            pltpu.VMEM((tile_rows, 8, 4 * STATE), BF16),
            pltpu.VMEM((tile_rows, 8, 2 * HEADS), BF16),
            dma((5,)),
            pltpu.VMEM((WINDOW, lines, 8, INNER), BF16),
            pltpu.VMEM((WINDOW, lines, 8, 4 * STATE), BF16),
            pltpu.VMEM((WINDOW, lines, 8, 2 * HEADS), BF16),
            pltpu.VMEM((WINDOW, lines, 8, INNER), BF16),
            pltpu.VMEM((tile_rows, 8, INNER), BF16),
            pltpu.VMEM((8, STATE, INNER), BF16),
            pltpu.VMEM((tall, STATE, INNER), BF16),
            pltpu.VMEM((8, 128), F32),
            pltpu.VMEM((tall, 8, 128), F32),
            pltpu.VMEM((tall, STATE, INNER), BF16),
            pltpu.VMEM((8, STATE, INNER), BF16),
            pltpu.VMEM((lines, STATE, INNER), BF16),
            pltpu.VMEM((lines, STATE, INNER), BF16),
            pltpu.VMEM((lines, STATE, INNER), BF16),
            pltpu.VMEM((lines, STATE, INNER), BF16),
            pltpu.VMEM((8, 128), F32),
            pltpu.VMEM((8, 128), F32),
            pltpu.VMEM((HEADS, tokens, tokens), BF16),
            pltpu.VMEM((tokens, INNER), F32),
            pltpu.VMEM((tokens, INNER), F32),
            pltpu.VMEM((tokens, INNER), F32),
            pltpu.VMEM((tokens, INNER), F32),
            pltpu.VMEM((tokens, INNER), F32),
            pltpu.VMEM((tokens, INNER), F32),
            dma((GROUPS,)),
            dma((GROUPS,)),
            dma((2,)),
            dma((2,)),
            dma((GROUPS,)),
            dma((GROUPS,)),
            dma((2,)),
            dma((2,)),
            dma,
            dma,
            dma((GROUPS,)),
            dma((GROUPS,)),
            dma((GROUPS,)),
            dma((GROUPS,)),
            dma,
            dma,
            pltpu.SemaphoreType.REGULAR,
        ],
        compiler_params=pltpu.CompilerParams(
            collective_id=0, has_side_effects=True, vmem_limit_bytes=60 * 1024 * 1024
        ),
    )(
        step_index,
        step_table.T,
        rates,
        skip.reshape(1, HEADS),
        norm_gain.reshape(INNER // 128, 128),
        x_in.reshape(tile_rows, 8, INNER),
        gate_in.reshape(tile_rows, 8, INNER),
        proj_bc.reshape(tile_rows, 8, 4 * STATE),
        dt_raw.reshape(tile_rows, 8, 2 * HEADS),
    )
    return out.reshape(x_in.shape)


def solution(mesh):
    tile = P("img", "row", "col", None)
    return jax.shard_map(
        functools.partial(body, mesh.shape["col"], mesh.shape["row"]),
        mesh=mesh,
        in_specs=(tile, tile, tile, tile, P("img"), P(), P(), P(), P()),
        out_specs=tile,
        check_vma=False,
    )
```
